128 devices in a mesh: seq: 8 (over z_lo, y), head: 16 (over x, z_hi, core).
Axes of the slice: x: 4, y: 4, z: 4 (z_hi: 2, z_lo: 2; z = z_hi * 2 + z_lo), core: 2. Of those that a mesh axis runs over, the one named last changes fastest.
Arguments:
- queries: bfloat16 [24576, 4096], P(('seq', 'head')), may hold values from -48 to 48
- keys: bfloat16 [24576, 2048], P(('seq', 'head')), may hold values from -4 to 4
- values: bfloat16 [24576, 2048], P(('seq', 'head')), may hold values from -6 to 6
- grad_out: bfloat16 [24576, 4096], P(('seq', 'head')), may hold values from -6 to 6
- doc_lengths: int32 [16], replicated, may hold values from 1 to 6144, 24576 in all
Outputs:
- grad_queries: bfloat16 [24576, 4096], P(('seq', 'head'))
- grad_keys: bfloat16 [24576, 2048], P(('seq', 'head'))
- grad_values: bfloat16 [24576, 2048], P(('seq', 'head'))
The draws below stay inside these ranges and needn't reach their ends.
Inputs may be any that keep to these rules, and one draw needn't show every extreme that they name: `doc_lengths`: the lengths sum to 24576.
All inputs are finite; a program needn't handle non-finite values.
Results may differ from the reference program's by a relative error of at most 0.012.
Values may be sent and summed in bfloat16 or wider, within the bound.
A program may use at most 128 MiB of HBM per device.

```python
import math
import jax
import jax.numpy as jnp
import numpy as np
from jax import lax

HEADS = 32
KV_HEADS = 16
HD = 128
WINDOW = 1024
QBLK = 512
DOCS = 16
TOKENS = 24576
DOC_MOST = 6144


def query_key_pair(key):
    key_query, key_keys = jax.random.split(jax.random.fold_in(key, 11), 2)
    q_shape = (TOKENS, HEADS, HD)
    k_shape = (TOKENS, KV_HEADS, HD)
    query_out = jax.random.truncated_normal(key_query, -4.0, 4.0, q_shape, jnp.float32)
    keys_out = jax.random.truncated_normal(key_keys, -4.0, 4.0, k_shape, jnp.float32)
    return (query_out.reshape(TOKENS, HEADS * HD), keys_out.reshape(TOKENS, KV_HEADS * HD))


def draw_queries(key, part):
    return query_key_pair(key)[0].astype(jnp.bfloat16)


def draw_keys(key, part):
    return query_key_pair(key)[1].astype(jnp.bfloat16)


def block_levels(stream_key, dims, cuts, smallest, high):
    def one(dim, blocks):
        heights = jax.random.uniform(jax.random.fold_in(jax.random.fold_in(stream_key, 6), dim), (blocks,), jnp.float32, smallest / len(cuts), high / len(cuts))
        return jnp.repeat(jnp.exp(heights), dims[dim] // blocks).reshape((-1,) + (1,) * (len(dims) - dim - 1))

    gain = one(*cuts[0])
    for cut in cuts[1:]:
        gain = gain * one(*cut)
    return gain


def split_up(count, total, reach, lean):
    weights = [(1 << 20) // math.isqrt(rank ** lean) + 1 for rank in range(2, count + 1)]
    rest, given = total - reach - (count - 1), [1] * (count - 1)
    while rest > 0:
        candidates = [i for i in range(count - 1) if given[i] < reach]
        pool, budget = sum([weights[i] for i in candidates]), rest
        for i in candidates:
            addition = min(reach - given[i], max(1, budget * weights[i] // pool), rest)
            given[i] = given[i] + addition
            rest = rest - addition
    return np.array([reach] + given)


def ragged(rng, amount, total, limit, slope):
    if amount == 2:
        one = jax.random.randint(rng, (), max(1, total - limit), min(limit, total - 1) + 1)
        return jnp.stack([one, total - one])
    sizes = jnp.asarray(split_up(amount, total, limit, slope), jnp.int32)
    twos = (amount - 1) // 2
    source_of, sink = sizes[1:1 + 2 * twos:2], sizes[2:2 + 2 * twos:2]
    slack = jnp.minimum(source_of - 1, limit - sink)
    passed = jax.random.randint(jax.random.fold_in(rng, 1), (twos,), 0, 1 << 20) % (slack + 1)
    sizes = sizes.at[1:1 + 2 * twos:2].set(source_of - passed).at[2:2 + 2 * twos:2].set(sink + passed)
    return sizes[jax.random.permutation(jax.random.fold_in(rng, 2), amount)]


def bell_draw(rng, shape, scale, reach, shards=(), kind=jnp.bfloat16):
    gain = block_levels(rng, shape, shards, -0.22, 0.18) if shards else 1.0
    drawn = jax.random.normal(rng, shape, jnp.float32) * scale * gain
    return jnp.minimum(jnp.maximum(drawn, -reach), reach).astype(kind)


def setup_inputs(seed: int = 0) -> dict:
    splits = jax.random.split(jax.random.key(seed), 6)
    queries = draw_queries(jax.random.fold_in(splits[5], 71), 0)
    keys = draw_keys(jax.random.fold_in(splits[5], 71), 0)
    values = bell_draw(splits[2], (TOKENS, KV_HEADS * HD), 1.0, 6.0, ((0, 128),))
    grad_out = bell_draw(splits[3], (TOKENS, HEADS * HD), 1.0, 6.0, ((0, 128),))
    doc_lengths = ragged(splits[4], DOCS, TOKENS, DOC_MOST, 1).astype(jnp.int32)
    return dict(queries=queries, keys=keys, values=values, grad_out=grad_out, doc_lengths=doc_lengths)


def doc_index(doc_lengths, positions):
    doc_ends = jnp.cumsum(doc_lengths).astype(jnp.int32)
    return jnp.sum((positions[:, None] >= doc_ends[None, :]).astype(jnp.int32), axis=1)


def tile_grads(q_rows, out_rows, key_rows, value_rows, allowed):
    scaling = HD ** -0.5
    row_count = q_rows.shape[0]
    kv_count = key_rows.shape[1]
    per_group = q_rows.shape[1] // kv_count
    q_four = q_rows.reshape(row_count, kv_count, per_group, HD).astype(jnp.float32)
    out_four = out_rows.reshape(row_count, kv_count, per_group, HD).astype(jnp.float32)
    key_float = key_rows.astype(jnp.float32)
    value_float = value_rows.astype(jnp.float32)
    scores = jnp.einsum("qagd,kad->agqk", q_four, key_float) * scaling
    scores = jnp.where(allowed[None, None], scores, -jnp.inf)
    row_max = jnp.max(scores, axis=3, keepdims=True)
    exponent = jnp.exp(scores - row_max)
    weights = exponent / jnp.sum(exponent, axis=3, keepdims=True)
    weights_b = weights.astype(jnp.bfloat16)
    grad_values = jnp.einsum("agqk,qagd->kad", weights_b.astype(jnp.float32), out_four)
    grad_weights = jnp.einsum("qagd,kad->agqk", out_four, value_float)
    row_dot = jnp.sum(weights * grad_weights, axis=3, keepdims=True)
    grad_scores = (weights * (grad_weights - row_dot) * scaling).astype(jnp.bfloat16)
    grad_query = jnp.einsum("agqk,kad->qagd", grad_scores.astype(jnp.float32), key_float)
    grad_keys = jnp.einsum("agqk,qagd->kad", grad_scores.astype(jnp.float32), q_four)
    return grad_query.reshape(row_count, kv_count * per_group, HD), grad_keys, grad_values


def reference(queries, keys, values, grad_out, doc_lengths):
    q_all = queries.reshape(TOKENS, HEADS, HD)
    out_all = grad_out.reshape(TOKENS, HEADS, HD)
    pad_rows = jnp.zeros((WINDOW, KV_HEADS, HD), jnp.bfloat16)
    key_ext = jnp.concatenate([pad_rows, keys.reshape(TOKENS, KV_HEADS, HD)], axis=0)
    value_ext = jnp.concatenate([pad_rows, values.reshape(TOKENS, KV_HEADS, HD)], axis=0)
    q_docs = doc_index(doc_lengths, jnp.arange(TOKENS, dtype=jnp.int32))
    k_docs = doc_index(doc_lengths, jnp.arange(TOKENS + WINDOW, dtype=jnp.int32) - WINDOW)
    span = QBLK + WINDOW
    q_iota = jnp.arange(QBLK, dtype=jnp.int32)
    k_iota = jnp.arange(span, dtype=jnp.int32)

    def advance(totals, block):
        key_total, value_total = totals
        first_row = (block * QBLK).astype(jnp.int32)
        q_rows = lax.dynamic_slice_in_dim(q_all, first_row, QBLK, 0)
        out_rows = lax.dynamic_slice_in_dim(out_all, first_row, QBLK, 0)
        key_rows = lax.dynamic_slice_in_dim(key_ext, first_row, span, 0)
        value_rows = lax.dynamic_slice_in_dim(value_ext, first_row, span, 0)
        q_pos = first_row + q_iota
        k_pos = first_row - WINDOW + k_iota
        q_doc = lax.dynamic_slice_in_dim(q_docs, first_row, QBLK, 0)
        k_doc = lax.dynamic_slice_in_dim(k_docs, first_row, span, 0)
        allowed = (q_doc[:, None] == k_doc[None, :]) & (k_pos[None, :] <= q_pos[:, None])
        allowed = allowed & (q_pos[:, None] - k_pos[None, :] < WINDOW) & (k_pos[None, :] >= 0)
        grad_query, grad_keys, grad_values = tile_grads(q_rows, out_rows, key_rows, value_rows, allowed)
        key_total = lax.dynamic_update_slice_in_dim(key_total, lax.dynamic_slice_in_dim(key_total, first_row, span, 0) + grad_keys, first_row, 0)
        value_total = lax.dynamic_update_slice_in_dim(value_total, lax.dynamic_slice_in_dim(value_total, first_row, span, 0) + grad_values, first_row, 0)
        return (key_total, value_total), grad_query

    zeros_ext = jnp.zeros((TOKENS + WINDOW, KV_HEADS, HD), jnp.float32)
    totals, grad_query = lax.scan(advance, (zeros_ext, zeros_ext), jnp.arange(TOKENS // QBLK, dtype=jnp.int32))
    grad_queries = grad_query.reshape(TOKENS, HEADS * HD).astype(jnp.bfloat16)
    grad_keys = totals[0][WINDOW:].reshape(TOKENS, KV_HEADS * HD).astype(jnp.bfloat16)
    grad_values = totals[1][WINDOW:].reshape(TOKENS, KV_HEADS * HD).astype(jnp.bfloat16)
    return grad_queries, grad_keys, grad_values
```

```python
import jax
import jax.numpy as jnp
from jax import lax
from jax.experimental import pallas as pl
from jax.experimental.pallas import tpu as pltpu
from jax.sharding import PartitionSpec as P

HD = 128
WINDOW = 1024
BQ = 256
BK = 256
NT=(WINDOW+BQ)//BK
SCALE=HD**-0.5
C2=SCALE*1.4426950408889634
NEG=-1e30
f32 = jnp.float32
bf16 = jnp.bfloat16
NTK=(((1,),(1,)),((),()))
NN=(((1,),(0,)),((),()))

def block(b, base, len_ref, q, do, k_ref, v_ref, kt_ref, dk_ref, dv_ref, s_scr, p_scr):
    first = base + b*BQ - WINDOW
    qi = lax.broadcasted_iota(jnp.int32,(1,BQ),1)
    gpos = first + WINDOW + qi
    end = jnp.int32(0)
    start = jnp.zeros((1,BQ),jnp.int32)
    for d in range(16):
        end = end + len_ref[d]
        start = jnp.where(gpos >= end, end, start)
    lo = jnp.maximum(qi+1, start-first)
    ki = lax.broadcasted_iota(jnp.int32,(BK,BQ),0)
    m = None
    for t in range(NT):
        r = pl.multiple_of(b*BQ + t*BK, BK)
        s = lax.dot_general(k_ref[pl.ds(r,BK),:], q, NTK, preferred_element_type=f32)
        ok = ki >= lo - t*BK
        if t==NT-1:
            ok = ok & (ki <= lax.broadcasted_iota(jnp.int32,(BK,BQ),1))
        s = jnp.where(ok, s, NEG)
        s_scr[t] = s
        mt = jnp.max(s.reshape(BK//8,8,BQ),axis=0)
        m = mt if m is None else jnp.maximum(m,mt)
    m = jnp.max(m,axis=0,keepdims=True)
    l = jnp.zeros((8,BQ),f32); dd = jnp.zeros((8,BQ),f32)
    for t in range(NT):
        r = pl.multiple_of(b*BQ + t*BK, BK)
        p = jnp.exp2((s_scr[t]-m)*C2)
        s_scr[t] = p
        dp = lax.dot_general(v_ref[pl.ds(r,BK),:], do, NTK, preferred_element_type=f32)
        p_scr[t] = dp
        l = l + jnp.sum(p.reshape(BK//8,8,BQ),axis=0)
        dd = dd + jnp.sum((p*dp).reshape(BK//8,8,BQ),axis=0)
    l = jnp.sum(l,axis=0,keepdims=True); dd = jnp.sum(dd,axis=0,keepdims=True)
    inv = 1.0/l
    dd = dd*inv
    dqt = None
    for t in range(NT):
        r = pl.multiple_of(b*BQ + t*BK, BK)
        w = s_scr[t]*inv
        ds = (w*(p_scr[t]-dd)).astype(bf16)
        dv_ref[pl.ds(r,BK),:] += lax.dot_general(w.astype(bf16), do, NN, preferred_element_type=f32)
        dk_ref[pl.ds(r,BK),:] += lax.dot_general(ds, q, NN, preferred_element_type=f32)
        x = lax.dot_general(kt_ref[:,pl.ds(r,BK)], ds, NN, preferred_element_type=f32)
        dqt = x if dqt is None else dqt + x
    return (dqt*SCALE).T


def attention_kernel(len_ref, q_ref, k_ref, v_ref, do_ref, dq_ref, dk_out, dv_out, kt, dk, dv, s_scr, p_scr):
    group = q_ref.shape[0]
    base = lax.axis_index("seq") * group

    def prepare(i, carry):
        r = pl.multiple_of(i * BK, BK)
        kt[:, pl.ds(r, BK)] = k_ref[pl.ds(r, BK), :].T
        dk[pl.ds(r, BK), :] = jnp.zeros((BK, HD), f32)
        dv[pl.ds(r, BK), :] = jnp.zeros((BK, HD), f32)
        return carry

    lax.fori_loop(0, k_ref.shape[0] // BK, prepare, 0)
    for h in range(q_ref.shape[1] // HD):
        cols = pl.ds(h * HD, HD)

        def tile(b, carry):
            r = pl.multiple_of(b * BQ, BQ)
            rows = pl.ds(r, BQ)
            q = q_ref[rows, cols]
            do = do_ref[rows, cols]
            grad = block(b, base, len_ref, q, do, k_ref, v_ref, kt, dk, dv, s_scr, p_scr)
            dq_ref[rows, cols] = grad.astype(bf16)
            return carry

        lax.fori_loop(0, group // BQ, tile, 0)
    dk_out[...] = (dk[...] * SCALE).astype(bf16)
    dv_out[...] = dv[...].astype(bf16)


def passed_along(shard, axis, by):
    count = lax.axis_size(axis)
    pairs = [(i, i + by) for i in range(count) if 0 <= i + by < count]
    return lax.ppermute(shard, axis, pairs)


def local(queries, keys, values, grad_out, doc_lengths):
    def heads(x):
        return lax.all_to_all(x, "head", split_axis=1, concat_axis=0, tiled=True)

    def tokens(x):
        return lax.all_to_all(x, "head", split_axis=0, concat_axis=1, tiled=True)

    q, k, v, do = heads(queries), heads(keys), heads(values), heads(grad_out)
    group = q.shape[0]
    rims = passed_along(jnp.concatenate([k[group - WINDOW :], v[group - WINDOW :]], axis=1), "seq", 1)
    k_ext = jnp.concatenate([rims[:, :HD], k], axis=0)
    v_ext = jnp.concatenate([rims[:, HD:], v], axis=0)
    vmem = pl.BlockSpec(memory_space=pltpu.VMEM)
    dq, dk, dv = pl.pallas_call(
        attention_kernel,
        out_shape=(
            jax.ShapeDtypeStruct(q.shape, bf16),
            jax.ShapeDtypeStruct(k_ext.shape, bf16),
            jax.ShapeDtypeStruct(v_ext.shape, bf16),
        ),
        in_specs=[pl.BlockSpec(memory_space=pltpu.SMEM), vmem, vmem, vmem, vmem],
        out_specs=(vmem, vmem, vmem),
        scratch_shapes=[
            pltpu.VMEM((HD, k_ext.shape[0]), bf16),
            pltpu.VMEM(k_ext.shape, f32),
            pltpu.VMEM(k_ext.shape, f32),
            pltpu.VMEM((NT, BK, BQ), f32),
            pltpu.VMEM((NT, BK, BQ), f32),
        ],
        compiler_params=pltpu.CompilerParams(vmem_limit_bytes=48 << 20),
    )(doc_lengths, q, k_ext, v_ext, do)
    back = passed_along(jnp.concatenate([dk[:WINDOW], dv[:WINDOW]], axis=1), "seq", -1).astype(f32)
    own = [dk[WINDOW:], dv[WINDOW:]]
    full = []
    for i, grad in enumerate(own):
        tail = grad[group - WINDOW :].astype(f32) + back[:, i * HD : (i + 1) * HD]
        full.append(jnp.concatenate([grad[: group - WINDOW], tail.astype(bf16)], axis=0))
    return tokens(dq), tokens(full[0]), tokens(full[1])


def solution(mesh):
    rows = P(("seq", "head"), None)
    return jax.shard_map(
        local,
        mesh=mesh,
        in_specs=(rows, rows, rows, rows, P()),
        out_specs=(rows, rows, rows),
        check_vma=False,
    )
```

```python
import functools
import jax
import jax.numpy as jnp
from jax import lax
from jax.experimental import pallas as pl
from jax.experimental.pallas import tpu as pltpu
from jax.sharding import PartitionSpec as P

HD = 128
WINDOW = 1024
BQ = 256
BK = 256
NT=(WINDOW+BQ)//BK
SCALE=HD**-0.5
C2=SCALE*1.4426950408889634
NEG=-1e30
f32 = jnp.float32
bf16 = jnp.bfloat16
NTK=(((1,),(1,)),((),()))
NN=(((1,),(0,)),((),()))

def block(b, base, len_ref, q, do, k_ref, v_ref, kt_ref, dk_ref, dv_ref, s_scr, p_scr):
    first = base + b*BQ - WINDOW
    qi = lax.broadcasted_iota(jnp.int32,(1,BQ),1)
    gpos = first + WINDOW + qi
    end = jnp.int32(0)
    start = jnp.zeros((1,BQ),jnp.int32)
    for d in range(16):
        end = end + len_ref[d]
        start = jnp.where(gpos >= end, end, start)
    lo = jnp.maximum(qi+1, start-first)
    ki = lax.broadcasted_iota(jnp.int32,(BK,BQ),0)
    m = None
    for t in range(NT):
        r = pl.multiple_of(b*BQ + t*BK, BK)
        s = lax.dot_general(k_ref[pl.ds(r,BK),:], q, NTK, preferred_element_type=f32)
        ok = ki >= lo - t*BK
        if t==NT-1:
            ok = ok & (ki <= lax.broadcasted_iota(jnp.int32,(BK,BQ),1))
        s = jnp.where(ok, s, NEG)
        s_scr[t] = s
        mt = jnp.max(s.reshape(BK//8,8,BQ),axis=0)
        m = mt if m is None else jnp.maximum(m,mt)
    m = jnp.max(m,axis=0,keepdims=True)
    l = jnp.zeros((8,BQ),f32); dd = jnp.zeros((8,BQ),f32)
    for t in range(NT):
        r = pl.multiple_of(b*BQ + t*BK, BK)
        p = jnp.exp2((s_scr[t]-m)*C2)
        s_scr[t] = p
        dp = lax.dot_general(v_ref[pl.ds(r,BK),:], do, NTK, preferred_element_type=f32)
        p_scr[t] = dp
        l = l + jnp.sum(p.reshape(BK//8,8,BQ),axis=0)
        dd = dd + jnp.sum((p*dp).reshape(BK//8,8,BQ),axis=0)
    l = jnp.sum(l,axis=0,keepdims=True); dd = jnp.sum(dd,axis=0,keepdims=True)
    inv = 1.0/l
    dd = dd*inv
    dqt = None
    for t in range(NT):
        r = pl.multiple_of(b*BQ + t*BK, BK)
        w = s_scr[t]*inv
        ds = (w*(p_scr[t]-dd)).astype(bf16)
        dv_ref[pl.ds(r,BK),:] += lax.dot_general(w.astype(bf16), do, NN, preferred_element_type=f32)
        dk_ref[pl.ds(r,BK),:] += lax.dot_general(ds, q, NN, preferred_element_type=f32)
        x = lax.dot_general(kt_ref[:,pl.ds(r,BK)], ds, NN, preferred_element_type=f32)
        dqt = x if dqt is None else dqt + x
    return (dqt*SCALE).T


def exchange_kernel(
    heads, groups,
    len_ref, q_hbm, k_hbm, v_hbm, do_hbm,
    dq_hbm, dk_hbm, dv_hbm,
    qb, dob, kx, vx, kt, dk, dv, dqo, dko, dvo, rk, rv, s_scr, p_scr,
    in_send, in_recv, out_send, out_recv, halo_send, halo_recv, rim_send, rim_recv,
):
    rows = q_hbm.shape[0]
    group = heads * rows
    tiles = group // BQ
    rim_tiles = WINDOW // BQ
    per = q_hbm.shape[1] // k_hbm.shape[1]
    me = lax.axis_index("head")
    seq = lax.axis_index("seq")
    base = seq * group
    MESH = pl.DeviceIdType.MESH

    def peer(t):
        return lax.rem(me + t, heads)

    barrier = pltpu.get_barrier_semaphore()

    def greet(t, c):
        pl.semaphore_signal(barrier, inc=1, device_id=(seq, peer(t)), device_id_type=MESH)
        return c

    lax.fori_loop(1, heads, greet, 0)

    for by in (1, groups - 1):
        near = lax.rem(seq + by, groups)
        pl.semaphore_signal(barrier, inc=1, device_id=(near, me), device_id_type=MESH)

    def source(kind, p):
        if kind == 0:
            return k_hbm.at[:, pl.ds(pl.multiple_of(p * HD, HD), HD)]
        if kind == 1:
            return v_hbm.at[:, pl.ds(pl.multiple_of(p * HD, HD), HD)]
        h = (kind - 2) // 2
        ref = q_hbm if kind % 2 == 0 else do_hbm
        return ref.at[:, pl.ds(pl.multiple_of((p * per + h) * HD, HD), HD)]

    def target(kind, j):
        own = pl.ds(pl.multiple_of(j * rows, 64), rows)
        if kind < 2:
            ref = kx if kind == 0 else vx
            return ref.at[pl.ds(pl.multiple_of(WINDOW + j * rows, 64), rows), :]
        ref = qb if kind % 2 == 0 else dob
        return ref.at[(kind - 2) // 2, own, :]

    kinds = 2 + 2 * per

    def in_copy(kind, t):
        p = peer(t)
        return pltpu.make_async_remote_copy(
            src_ref=source(kind, p), dst_ref=target(kind, me),
            send_sem=in_send.at[kind, t], recv_sem=in_recv.at[kind, me],
            device_id=(seq, p), device_id_type=MESH,
        )

    def own_copy(kind):
        return pltpu.make_async_copy(source(kind, me), target(kind, me), in_recv.at[kind, me])

    def arrived(kind, j):
        pltpu.make_async_copy(target(kind, j), target(kind, j), in_recv.at[kind, j]).wait()

    for kind in range(kinds):
        own_copy(kind).start()

    def clear(i, c):
        r = pl.multiple_of(i * BK, BK)
        dk[pl.ds(r, BK), :] = jnp.zeros((BK, HD), f32)
        dv[pl.ds(r, BK), :] = jnp.zeros((BK, HD), f32)
        return c

    lax.fori_loop(0, (WINDOW + group) // BK, clear, 0)

    pl.semaphore_wait(barrier, heads + 1)

    for first in range(0, kinds, 2):
        def send(t, c):
            in_copy(first, t).start()
            in_copy(first + 1, t).start()
            return c

        lax.fori_loop(1, heads, send, 0)

    def halo(i):
        ref = kx if i == 0 else vx
        return pltpu.make_async_remote_copy(
            src_ref=ref.at[pl.ds(group, WINDOW), :], dst_ref=ref.at[pl.ds(0, WINDOW), :],
            send_sem=halo_send.at[i], recv_sem=halo_recv.at[i],
            device_id=(seq + 1, me), device_id_type=MESH,
        )

    def kv_wait(j, c):
        arrived(0, j)
        arrived(1, j)
        return c

    late = (group - WINDOW) // rows
    lax.fori_loop(late, heads, kv_wait, 0)

    @pl.when(seq < groups - 1)
    def _():
        halo(0).start()
        halo(1).start()

    lax.fori_loop(0, late, kv_wait, 0)

    def turn(i, c):
        r = pl.multiple_of(i * BK, BK)
        kt[:, pl.ds(r, BK)] = kx[pl.ds(r, BK), :].T
        return c

    lax.fori_loop(WINDOW // BK, (WINDOW + group) // BK, turn, 0)

    @pl.when(seq == 0)
    def _():
        kx[pl.ds(0, WINDOW), :] = jnp.zeros((WINDOW, HD), bf16)
        vx[pl.ds(0, WINDOW), :] = jnp.zeros((WINDOW, HD), bf16)

    @pl.when(seq > 0)
    def _():
        for i, ref in enumerate((kx, vx)):
            own = ref.at[pl.ds(0, WINDOW), :]
            pltpu.make_async_copy(own, own, halo_recv.at[i]).wait()

    lax.fori_loop(0, WINDOW // BK, turn, 0)

    def out_parts(kind, h, j):
        own = pl.ds(pl.multiple_of(j * rows, 64), rows)
        ext = pl.ds(pl.multiple_of(WINDOW + j * rows, 64), rows)
        if kind == 0:
            col = pl.ds(pl.multiple_of((me * per + h) * HD, HD), HD)
            return dqo.at[h, own, :], dq_hbm.at[:, col], h
        col = pl.ds(pl.multiple_of(me * HD, HD), HD)
        if kind == 1:
            return dko.at[ext, :], dk_hbm.at[:, col], per
        return dvo.at[ext, :], dv_hbm.at[:, col], per + 1

    def out_copy(kind, h, j):
        src, dst, row = out_parts(kind, h, j)
        return pltpu.make_async_remote_copy(
            src_ref=src, dst_ref=dst,
            send_sem=out_send.at[row, j], recv_sem=out_recv.at[row, me],
            device_id=(seq, j), device_id_type=MESH,
        )

    def out_own(kind, h):
        src, dst, row = out_parts(kind, h, me)
        return pltpu.make_async_copy(src, dst, out_recv.at[row, me])

    def deliver(kind, h, lo, hi):
        def one(j, c):
            @pl.when(j != me)
            def _():
                out_copy(kind, h, j).start()

            @pl.when(j == me)
            def _():
                out_own(kind, h).start()

            return c

        lax.fori_loop(lo, hi, one, 0)

    def rim(i, b):
        src = (dko, dvo)[i].at[pl.ds(pl.multiple_of(b * BQ, BQ), BQ), :]
        dst = (rk, rv)[i].at[pl.ds(pl.multiple_of(b * BQ, BQ), BQ), :]
        return pltpu.make_async_remote_copy(
            src_ref=src, dst_ref=dst,
            send_sem=rim_send.at[i, b], recv_sem=rim_recv.at[i, b],
            device_id=(seq - 1, me), device_id_type=MESH,
        )

    def step(it, c):
        h = it // tiles
        b = lax.rem(it, tiles)
        r = pl.multiple_of(b * BQ, BQ)

        def wait_rows(j, c):
            own = pl.ds(pl.multiple_of(j * rows, 64), rows)
            for i, ref in enumerate((qb, dob)):
                view = ref.at[h, own, :]
                pltpu.make_async_copy(view, view, in_recv.at[2 + 2 * h + i, j]).wait()
            return c

        lax.fori_loop((BQ * b + rows - 1) // rows, (BQ * b + BQ - 1) // rows + 1, wait_rows, 0)
        q = qb[h, pl.ds(r, BQ), :]
        do = dob[h, pl.ds(r, BQ), :]
        grad = block(b, base, len_ref, q, do, kx, vx, kt, dk, dv, s_scr, p_scr)
        dqo[h, pl.ds(r, BQ), :] = grad.astype(bf16)
        deliver(0, h, BQ * b // rows, BQ * (b + 1) // rows)

        @pl.when(h == per - 1)
        def _():
            dko[pl.ds(r, BQ), :] = (dk[pl.ds(r, BQ), :] * SCALE).astype(bf16)
            dvo[pl.ds(r, BQ), :] = dv[pl.ds(r, BQ), :].astype(bf16)

            @pl.when((b < rim_tiles) & (seq > 0))
            def _():
                rim(0, b).start()
                rim(1, b).start()

            @pl.when(b >= rim_tiles)
            def _():
                o = b - rim_tiles
                for kind in (1, 2):
                    deliver(kind, 0, BQ * o // rows, BQ * (o + 1) // rows)

        return c

    lax.fori_loop(0, per * tiles, step, 0)

    def last(i, c):
        r = pl.multiple_of(group + i * BQ, BQ)
        o = pl.multiple_of(i * BQ, BQ)

        @pl.when(seq < groups - 1)
        def _():
            for n, ref in enumerate((rk, rv)):
                view = ref.at[pl.ds(o, BQ), :]
                pltpu.make_async_copy(view, view, rim_recv.at[n, i]).wait()
            dko[pl.ds(r, BQ), :] = (dk[pl.ds(r, BQ), :] * SCALE + rk[pl.ds(o, BQ), :].astype(f32)).astype(bf16)
            dvo[pl.ds(r, BQ), :] = (dv[pl.ds(r, BQ), :] + rv[pl.ds(o, BQ), :].astype(f32)).astype(bf16)

        @pl.when(seq == groups - 1)
        def _():
            dko[pl.ds(r, BQ), :] = (dk[pl.ds(r, BQ), :] * SCALE).astype(bf16)
            dvo[pl.ds(r, BQ), :] = dv[pl.ds(r, BQ), :].astype(bf16)

        b = tiles - rim_tiles + i
        for kind in (1, 2):
            deliver(kind, 0, BQ * b // rows, BQ * (b + 1) // rows)
        return c

    lax.fori_loop(0, rim_tiles, last, 0)

    def finish(t, c):
        p = peer(t)
        for kind in range(kinds):
            in_copy(kind, t).wait_send()
        for h in range(per):
            out_copy(0, h, p).wait_send()
        out_copy(1, 0, p).wait_send()
        out_copy(2, 0, p).wait_send()
        return c

    lax.fori_loop(1, heads, finish, 0)

    def landed(j, c):
        for row in range(per + 2):
            ref = dq_hbm if row < per else (dk_hbm, dv_hbm)[row - per]
            col = (j * per + row) * HD if row < per else j * HD
            view = ref.at[:, pl.ds(pl.multiple_of(col, HD), HD)]
            pltpu.make_async_copy(view, view, out_recv.at[row, j]).wait()
        return c

    lax.fori_loop(0, heads, landed, 0)

    @pl.when(seq < groups - 1)
    def _():
        halo(0).wait_send()
        halo(1).wait_send()

    @pl.when(seq > 0)
    def _():
        for b in range(rim_tiles):
            rim(0, b).wait_send()
            rim(1, b).wait_send()


def local(queries, keys, values, grad_out, doc_lengths):
    heads, groups = lax.axis_size("head"), lax.axis_size("seq")
    rows = queries.shape[0]
    group = heads * rows
    ext = group + WINDOW
    per = queries.shape[1] // keys.shape[1]
    hbm = pl.BlockSpec(memory_space=pl.ANY)
    dma = pltpu.SemaphoreType.DMA
    return pl.pallas_call(
        functools.partial(exchange_kernel, heads, groups),
        out_shape=(
            jax.ShapeDtypeStruct(queries.shape, bf16),
            jax.ShapeDtypeStruct(keys.shape, bf16),
            jax.ShapeDtypeStruct(values.shape, bf16),
        ),
        in_specs=[pl.BlockSpec(memory_space=pltpu.SMEM), hbm, hbm, hbm, hbm],
        out_specs=(hbm, hbm, hbm),
        scratch_shapes=[
            pltpu.VMEM((per, group, HD), bf16),
            pltpu.VMEM((per, group, HD), bf16),
            pltpu.VMEM((ext, HD), bf16),
            pltpu.VMEM((ext, HD), bf16),
            pltpu.VMEM((HD, ext), bf16),
            pltpu.VMEM((ext, HD), f32),
            pltpu.VMEM((ext, HD), f32),
            pltpu.VMEM((per, group, HD), bf16),
            pltpu.VMEM((ext, HD), bf16),
            pltpu.VMEM((ext, HD), bf16),
            pltpu.VMEM((WINDOW, HD), bf16),
            pltpu.VMEM((WINDOW, HD), bf16),
            pltpu.VMEM((NT, BK, BQ), f32),
            pltpu.VMEM((NT, BK, BQ), f32),
            dma((2 + 2 * per, heads)),
            dma((2 + 2 * per, heads)),
            dma((2 + per, heads)),
            dma((2 + per, heads)),
            dma((2,)),
            dma((2,)),
            dma((2, WINDOW // BQ)),
            dma((2, WINDOW // BQ)),
        ],
        compiler_params=pltpu.CompilerParams(
            collective_id=0, has_side_effects=True, vmem_limit_bytes=48 << 20
        ),
    )(doc_lengths, queries, keys, values, grad_out)


def solution(mesh):
    rows = P(("seq", "head"), None)
    return jax.shard_map(
        local,
        mesh=mesh,
        in_specs=(rows, rows, rows, rows, P()),
        out_specs=(rows, rows, rows),
        check_vma=False,
    )
```

```python
import functools

import jax
import jax.numpy as jnp
from jax import lax
from jax.experimental import pallas as pl
from jax.experimental.pallas import tpu as pltpu
from jax.sharding import PartitionSpec as P

HD = 128
WINDOW = 1024
BQ = 256
BK = 256
NT=(WINDOW+BQ)//BK
SCALE=HD**-0.5
C2=SCALE*1.4426950408889634
NEG=-1e30
f32 = jnp.float32
bf16 = jnp.bfloat16
NTK=(((1,),(1,)),((),()))
NN=(((1,),(0,)),((),()))
def block(b, base, len_ref, qs, dos, k_ref, v_ref, kt_ref, dk_ref, dv_ref, s_scr, p_scr):
    per=len(qs)
    first = base + b*BQ - WINDOW
    qi = lax.broadcasted_iota(jnp.int32,(1,BQ),1)
    gpos = first + WINDOW + qi
    end = jnp.int32(0)
    start = jnp.zeros((1,BQ),jnp.int32)
    for d in range(16):
        end = end + len_ref[d]
        start = jnp.where(gpos >= end, end, start)
    lo = jnp.maximum(qi+1, start-first)
    ki = lax.broadcasted_iota(jnp.int32,(BK,BQ),0)
    rows=[pl.ds(pl.multiple_of(b*BQ + t*BK, BK),BK) for t in range(NT)]
    stats=[]
    for h in range(per):
        q,do=qs[h],dos[h]
        m = None
        for t in range(NT):
            s = lax.dot_general(k_ref[rows[t],:], q, NTK, preferred_element_type=f32)
            ok = ki >= lo - t*BK
            if t==NT-1:
                ok = ok & (ki <= lax.broadcasted_iota(jnp.int32,(BK,BQ),1))
            s = jnp.where(ok, s, NEG)
            s_scr[h,t] = s
            mt = jnp.max(s.reshape(BK//8,8,BQ),axis=0)
            m = mt if m is None else jnp.maximum(m,mt)
        m = jnp.max(m,axis=0,keepdims=True)
        l = jnp.zeros((8,BQ),f32); dd = jnp.zeros((8,BQ),f32)
        for t in range(NT):
            p = jnp.exp2((s_scr[h,t]-m)*C2)
            s_scr[h,t] = p
            dp = lax.dot_general(v_ref[rows[t],:], do, NTK, preferred_element_type=f32)
            p_scr[h,t] = dp
            l = l + jnp.sum(p.reshape(BK//8,8,BQ),axis=0)
            dd = dd + jnp.sum((p*dp).reshape(BK//8,8,BQ),axis=0)
        l = jnp.sum(l,axis=0,keepdims=True); dd = jnp.sum(dd,axis=0,keepdims=True)
        inv = 1.0/l
        stats.append((inv,dd*inv))
    dqt = [None]*per
    q_all=jnp.concatenate(qs,axis=0); do_all=jnp.concatenate(dos,axis=0)
    for t in range(NT):
        ws=[];dss=[]
        for h in range(per):
            inv,dd=stats[h]
            w = s_scr[h,t]*inv
            ds = (w*(p_scr[h,t]-dd)).astype(bf16)
            ws.append(w.astype(bf16)); dss.append(ds)
            x = lax.dot_general(kt_ref[:,rows[t]], ds, NN, preferred_element_type=f32)
            dqt[h] = x if dqt[h] is None else dqt[h] + x
        dv_ref[rows[t],:] += lax.dot_general(jnp.concatenate(ws,axis=1), do_all, NN, preferred_element_type=f32)
        dk_ref[rows[t],:] += lax.dot_general(jnp.concatenate(dss,axis=1), q_all, NN, preferred_element_type=f32)
    return [(x*SCALE).T for x in dqt]


def exchange_kernel(
    heads, groups,
    len_ref, q_hbm, k_hbm, v_hbm, do_hbm,
    dq_hbm, dk_hbm, dv_hbm,
    qb, dob, kx, vx, kt, dk, dv, dqo, dko, dvo, rk, rv, s_scr, p_scr,
    in_send, in_recv, out_send, out_recv, halo_send, halo_recv, rim_send, rim_recv,
):
    rows = q_hbm.shape[0]
    group = heads * rows
    tiles = group // BQ
    per = q_hbm.shape[1] // k_hbm.shape[1]
    wide = per * HD
    me = lax.axis_index("head")
    seq = lax.axis_index("seq")
    base = seq * group
    MESH = pl.DeviceIdType.MESH

    quads = heads // 4
    per_quad = tiles // quads
    mine, place = me // 4, lax.rem(me, 4)
    start = lax.rem(mine + 1 + place, quads)

    def quad_at(n):
        return lax.rem(start + n, quads)

    def receiver(i):
        to = lax.rem(place + lax.rem(i, 4), 4)
        return lax.rem(mine + 3 * quads - 1 - to - i // 4, quads) * 4 + to

    def peer(t):
        return lax.rem(me + t, heads)

    half = groups // 2

    def traded(p, yes):
        return p + lax.rem(p, 2) * yes * (2 - 4 * lax.rem(p // 2, 2))

    def head_of(p):
        return traded(p, seq // half)

    after = lax.rem(seq + 1, groups)
    before = lax.rem(seq + groups - 1, groups)
    next_id = (after, traded(me, lax.rem(seq // half + after // half, 2)))
    prev_id = (before, traded(me, lax.rem(seq // half + before // half, 2)))

    barrier = pltpu.get_barrier_semaphore()

    def greet(t, c):
        pl.semaphore_signal(barrier, inc=1, device_id=(seq, peer(t)), device_id_type=MESH)
        return c

    lax.fori_loop(1, heads, greet, 0)
    for near in (next_id, prev_id):
        pl.semaphore_signal(barrier, inc=1, device_id=near, device_id_type=MESH)

    sources = (k_hbm, v_hbm, q_hbm, do_hbm)
    targets = (kx, vx, qb, dob)
    widths = (HD, HD, wide, wide)

    def target(kind, j):
        first = j * rows + (WINDOW if kind < 2 else 0)
        return targets[kind].at[pl.ds(pl.multiple_of(first, 64), rows), :]

    def source(kind, p):
        w = widths[kind]
        return sources[kind].at[:, pl.ds(pl.multiple_of(head_of(p) * w, w), w)]

    def in_copy(kind, p):
        return pltpu.make_async_remote_copy(
            src_ref=source(kind, p), dst_ref=target(kind, me),
            send_sem=in_send.at[kind, p], recv_sem=in_recv.at[kind, me],
            device_id=(seq, p), device_id_type=MESH,
        )

    def arrived(kind, j):
        pltpu.make_async_copy(target(kind, j), target(kind, j), in_recv.at[kind, j]).wait()

    for kind in range(4):
        pltpu.make_async_copy(source(kind, me), target(kind, me), in_recv.at[kind, me]).start()

    def clear(i, c):
        r = pl.multiple_of(i * BK, BK)
        dk[pl.ds(r, BK), :] = jnp.zeros((BK, HD), f32)
        dv[pl.ds(r, BK), :] = jnp.zeros((BK, HD), f32)
        return c

    lax.fori_loop(0, (WINDOW + group) // BK, clear, 0)

    pl.semaphore_wait(barrier, heads + 1)

    for first in (0, 2):
        def send(i, c):
            p = receiver(i)

            @pl.when(p != me)
            def _():
                in_copy(first, p).start()
                in_copy(first + 1, p).start()

            return c

        lax.fori_loop(0, heads, send, 0)

    def halo(i):
        ref = (kx, vx)[i]
        return pltpu.make_async_remote_copy(
            src_ref=ref.at[pl.ds(group, WINDOW), :], dst_ref=ref.at[pl.ds(0, WINDOW), :],
            send_sem=halo_send.at[i], recv_sem=halo_recv.at[i],
            device_id=next_id, device_id_type=MESH,
        )

    def kv_wait(j, c):
        arrived(0, j)
        arrived(1, j)
        return c

    late = (group - WINDOW) // rows
    lax.fori_loop(late, heads, kv_wait, 0)

    @pl.when(seq < groups - 1)
    def _():
        halo(0).start()
        halo(1).start()

    lax.fori_loop(0, late, kv_wait, 0)

    def turn(i, c):
        r = pl.multiple_of(i * BK, BK)
        kt[:, pl.ds(r, BK)] = kx[pl.ds(r, BK), :].T
        return c

    lax.fori_loop(WINDOW // BK, (WINDOW + group) // BK, turn, 0)

    def halo_wait():
        @pl.when(seq == 0)
        def _():
            kx[pl.ds(0, WINDOW), :] = jnp.zeros((WINDOW, HD), bf16)
            vx[pl.ds(0, WINDOW), :] = jnp.zeros((WINDOW, HD), bf16)

        @pl.when(seq > 0)
        def _():
            for i, ref in enumerate((kx, vx)):
                own = ref.at[pl.ds(0, WINDOW), :]
                pltpu.make_async_copy(own, own, halo_recv.at[i]).wait()

        lax.fori_loop(0, WINDOW // BK, turn, 0)

    staged = (dqo, dko, dvo)
    results = (dq_hbm, dk_hbm, dv_hbm)

    def out_parts(kind, j):
        first = j * rows + (WINDOW if kind else 0)
        w = HD if kind else wide
        src = staged[kind].at[pl.ds(pl.multiple_of(first, 64), rows), :]
        return src, results[kind].at[:, pl.ds(pl.multiple_of(head_of(me) * w, w), w)]

    def out_copy(kind, j):
        src, dst = out_parts(kind, j)
        return pltpu.make_async_remote_copy(
            src_ref=src, dst_ref=dst,
            send_sem=out_send.at[kind, j], recv_sem=out_recv.at[kind, me],
            device_id=(seq, j), device_id_type=MESH,
        )

    def deliver(kinds, lo, count):
        def one(i, c):
            j = lo + lax.rem(i + place, count)
            for kind in kinds:
                @pl.when(j != me)
                def _():
                    out_copy(kind, j).start()

                @pl.when(j == me)
                def _():
                    src, dst = out_parts(kind, me)
                    pltpu.make_async_copy(src, dst, out_recv.at[kind, me]).start()

            return c

        lax.fori_loop(0, count, one, 0)

    def rim(i):
        return pltpu.make_async_remote_copy(
            src_ref=(dko, dvo)[i].at[pl.ds(0, WINDOW), :], dst_ref=(rk, rv)[i],
            send_sem=rim_send.at[i], recv_sem=rim_recv.at[i],
            device_id=prev_id, device_id_type=MESH,
        )

    def stage(lo, count):
        def one(i, c):
            r = pl.multiple_of(lo + i * 128, 128)
            dko[pl.ds(r, 128), :] = (dk[pl.ds(r, 128), :] * SCALE).astype(bf16)
            dvo[pl.ds(r, 128), :] = dv[pl.ds(r, 128), :].astype(bf16)
            return c

        lax.fori_loop(0, count // 128, one, 0)

    def at_stage(y, over):
        off = lax.rem(y - start + 2 * quads, quads)
        return jnp.where(off + over < quads, off + over, quads - 1)

    def step(n, c):
        quad = quad_at(n)

        def rows_wait(j, c):
            arrived(2, j)
            arrived(3, j)
            return c

        lax.fori_loop(quad * 4, quad * 4 + 4, rows_wait, 0)

        def tile(i, c):
            b = quad * per_quad + lax.rem(i + 1, per_quad)
            first_use = jnp.where(start == 1, per_quad, 1)

            @pl.when(b == first_use)
            def _():
                halo_wait()

            r = pl.multiple_of(b * BQ, BQ)
            qs = [qb[pl.ds(r, BQ), h * HD : (h + 1) * HD] for h in range(per)]
            dos = [dob[pl.ds(r, BQ), h * HD : (h + 1) * HD] for h in range(per)]
            grads = block(b, base, len_ref, qs, dos, kx, vx, kt, dk, dv, s_scr, p_scr)
            for h in range(per):
                dqo[pl.ds(r, BQ), h * HD : (h + 1) * HD] = grads[h].astype(bf16)
            return c

        lax.fori_loop(0, per_quad, tile, 0)
        deliver((0,), quad * 4, 4)

        @pl.when(n == at_stage(0, 1))
        def _():
            @pl.when(seq > 0)
            def _():
                stage(0, WINDOW)
                rim(0).start()
                rim(1).start()

        for y, count in ((0, 4), (1, 4), (2, late - 8)):
            @pl.when(n == at_stage(y, min(2, quads - 1 - y)))
            def _():
                stage(WINDOW + y * 4 * rows, count * rows)
                deliver((1, 2), y * 4, count)

        return c

    lax.fori_loop(0, quads, step, 0)

    @pl.when(seq < groups - 1)
    def _():
        for i, ref in enumerate((rk, rv)):
            pltpu.make_async_copy(ref, ref, rim_recv.at[i]).wait()

    def last(i, c):
        r = pl.multiple_of(group + i * 128, 128)
        o = pl.multiple_of(i * 128, 128)

        @pl.when(seq < groups - 1)
        def _():
            dk[pl.ds(r, 128), :] += rk[pl.ds(o, 128), :].astype(f32) * (1.0 / SCALE)
            dv[pl.ds(r, 128), :] += rv[pl.ds(o, 128), :].astype(f32)

        return c

    lax.fori_loop(0, WINDOW // 128, last, 0)
    stage(WINDOW + late * rows, (heads - late) * rows)
    deliver((1, 2), late, heads - late)

    def finish(t, c):
        p = peer(t)
        for kind in range(4):
            in_copy(kind, p).wait_send()
        for kind in range(3):
            out_copy(kind, p).wait_send()
        return c

    lax.fori_loop(1, heads, finish, 0)

    def landed(j, c):
        for kind in range(3):
            w = HD if kind else wide
            view = results[kind].at[:, pl.ds(pl.multiple_of(head_of(j) * w, w), w)]
            pltpu.make_async_copy(view, view, out_recv.at[kind, j]).wait()
        return c

    lax.fori_loop(0, heads, landed, 0)

    @pl.when(seq < groups - 1)
    def _():
        halo(0).wait_send()
        halo(1).wait_send()

    @pl.when(seq > 0)
    def _():
        rim(0).wait_send()
        rim(1).wait_send()


def local(queries, keys, values, grad_out, doc_lengths):
    heads, groups = lax.axis_size("head"), lax.axis_size("seq")
    rows = queries.shape[0]
    group = heads * rows
    ext = group + WINDOW
    per = queries.shape[1] // keys.shape[1]
    hbm = pl.BlockSpec(memory_space=pl.ANY)
    dma = pltpu.SemaphoreType.DMA
    return pl.pallas_call(
        functools.partial(exchange_kernel, heads, groups),
        out_shape=(
            jax.ShapeDtypeStruct(queries.shape, bf16),
            jax.ShapeDtypeStruct(keys.shape, bf16),
            jax.ShapeDtypeStruct(values.shape, bf16),
        ),
        in_specs=[pl.BlockSpec(memory_space=pltpu.SMEM), hbm, hbm, hbm, hbm],
        out_specs=(hbm, hbm, hbm),
        scratch_shapes=[
            pltpu.VMEM((group, per * HD), bf16),
            pltpu.VMEM((group, per * HD), bf16),
            pltpu.VMEM((ext, HD), bf16),
            pltpu.VMEM((ext, HD), bf16),
            pltpu.VMEM((HD, ext), bf16),
            pltpu.VMEM((ext, HD), f32),
            pltpu.VMEM((ext, HD), f32),
            pltpu.VMEM((group, per * HD), bf16),
            pltpu.VMEM((ext, HD), bf16),
            pltpu.VMEM((ext, HD), bf16),
            pltpu.VMEM((WINDOW, HD), bf16),
            pltpu.VMEM((WINDOW, HD), bf16),
            pltpu.VMEM((per, NT, BK, BQ), f32),
            pltpu.VMEM((per, NT, BK, BQ), f32),
            dma((4, heads)),
            dma((4, heads)),
            dma((3, heads)),
            dma((3, heads)),
            dma((2,)),
            dma((2,)),
            dma((2,)),
            dma((2,)),
        ],
        compiler_params=pltpu.CompilerParams(
            collective_id=0, has_side_effects=True, vmem_limit_bytes=60 << 20
        ),
    )(doc_lengths, queries, keys, values, grad_out)


def solution(mesh):
    rows = P(("seq", "head"), None)
    return jax.shard_map(
        local,
        mesh=mesh,
        in_specs=(rows, rows, rows, rows, P()),
        out_specs=(rows, rows, rows),
        check_vma=False,
    )
```

```python
import functools

import jax
import jax.numpy as jnp
from jax import lax
from jax.experimental import pallas as pl
from jax.experimental.pallas import tpu as pltpu
from jax.sharding import PartitionSpec as P

HD = 128
WINDOW = 1024
BQ = 256
BK = 256
NT=(WINDOW+BQ)//BK
SCALE=HD**-0.5
C2=SCALE*1.4426950408889634
NEG=-1e30
f32 = jnp.float32
bf16 = jnp.bfloat16
NTK=(((1,),(1,)),((),()))
NN=(((1,),(0,)),((),()))
def block(b, base, len_ref, qs, dos, k_ref, v_ref, kt_ref, dk_ref, dv_ref, s_scr, p_scr):
    per=len(qs)
    first = base + b*BQ - WINDOW
    qi = lax.broadcasted_iota(jnp.int32,(1,BQ),1)
    gpos = first + WINDOW + qi
    end = jnp.int32(0)
    start = jnp.zeros((1,BQ),jnp.int32)
    for d in range(16):
        end = end + len_ref[d]
        start = jnp.where(gpos >= end, end, start)
    lo = jnp.maximum(qi+1, start-first)
    ki = lax.broadcasted_iota(jnp.int32,(BK,BQ),0)
    rows=[pl.ds(pl.multiple_of(b*BQ + t*BK, BK),BK) for t in range(NT)]
    stats=[]
    for h in range(per):
        q,do=qs[h],dos[h]
        m = None
        for t in range(NT):
            s = lax.dot_general(k_ref[rows[t],:], q, NTK, preferred_element_type=f32)
            ok = ki >= lo - t*BK
            if t==NT-1:
                ok = ok & (ki <= lax.broadcasted_iota(jnp.int32,(BK,BQ),1))
            s = jnp.where(ok, s, NEG)
            s_scr[h,t] = s
            mt = jnp.max(s.reshape(BK//8,8,BQ),axis=0)
            m = mt if m is None else jnp.maximum(m,mt)
        m = jnp.max(m,axis=0,keepdims=True)
        l = jnp.zeros((8,BQ),f32); dd = jnp.zeros((8,BQ),f32)
        for t in range(NT):
            p = jnp.exp2((s_scr[h,t]-m)*C2)
            s_scr[h,t] = p
            dp = lax.dot_general(v_ref[rows[t],:], do, NTK, preferred_element_type=f32)
            p_scr[h,t] = dp
            l = l + jnp.sum(p.reshape(BK//8,8,BQ),axis=0)
            dd = dd + jnp.sum((p*dp).reshape(BK//8,8,BQ),axis=0)
        l = jnp.sum(l,axis=0,keepdims=True); dd = jnp.sum(dd,axis=0,keepdims=True)
        inv = 1.0/l
        stats.append((inv,dd*inv))
    dqt = [None]*per
    q_all=jnp.concatenate(qs,axis=0); do_all=jnp.concatenate(dos,axis=0)
    for t in range(NT):
        ws=[];dss=[]
        for h in range(per):
            inv,dd=stats[h]
            w = s_scr[h,t]*inv
            ds = (w*(p_scr[h,t]-dd)).astype(bf16)
            ws.append(w.astype(bf16)); dss.append(ds)
            x = lax.dot_general(kt_ref[:,rows[t]], ds, NN, preferred_element_type=f32)
            dqt[h] = x if dqt[h] is None else dqt[h] + x
        dv_ref[rows[t],:] += lax.dot_general(jnp.concatenate(ws,axis=1), do_all, NN, preferred_element_type=f32)
        dk_ref[rows[t],:] += lax.dot_general(jnp.concatenate(dss,axis=1), q_all, NN, preferred_element_type=f32)
    return [(x*SCALE).T for x in dqt]


def exchange_kernel(
    heads, groups,
    len_ref, q_hbm, k_hbm, v_hbm, do_hbm,
    dq_hbm, dk_hbm, dv_hbm,
    qb, dob, kx, vx, kt, dk, dv, dqo, dko, dvo, rk, rv, s_scr, p_scr,
    in_send, in_recv, out_send, out_recv, halo_send, halo_recv, rim_send, rim_recv,
):
    rows = q_hbm.shape[0]
    group = heads * rows
    tiles = group // BQ
    per = q_hbm.shape[1] // k_hbm.shape[1]
    wide = per * HD
    me = lax.axis_index("head")
    seq = lax.axis_index("seq")
    base = seq * group
    MESH = pl.DeviceIdType.MESH

    quads = heads // 4
    per_quad = tiles // quads
    mine, place = me // 4, lax.rem(me, 4)
    start = lax.rem(mine + 1 + place, quads)

    def quad_at(n):
        return lax.rem(start + n, quads)

    def receiver(i):
        to = lax.rem(place + lax.rem(i, 4), 4)
        return lax.rem(mine + 3 * quads - 1 - to - i // 4, quads) * 4 + to

    def peer(t):
        return lax.rem(me + t, heads)

    half = groups // 2

    def traded(p, yes):
        return p + lax.rem(p, 2) * yes * (2 - 4 * lax.rem(p // 2, 2))

    def head_of(p):
        return traded(p, seq // half)

    after = lax.rem(seq + 1, groups)
    before = lax.rem(seq + groups - 1, groups)
    next_id = (after, traded(me, lax.rem(seq // half + after // half, 2)))
    prev_id = (before, traded(me, lax.rem(seq // half + before // half, 2)))

    barrier = pltpu.get_barrier_semaphore()

    def greet(t, c):
        pl.semaphore_signal(barrier, inc=1, device_id=(seq, peer(t)), device_id_type=MESH)
        return c

    lax.fori_loop(1, heads, greet, 0)
    for near in (next_id, prev_id):
        pl.semaphore_signal(barrier, inc=1, device_id=near, device_id_type=MESH)

    sources = (k_hbm, v_hbm, q_hbm, do_hbm)
    targets = (kx, vx, qb, dob)
    widths = (HD, HD, wide, wide)

    def target(kind, j):
        first = j * rows + (WINDOW if kind < 2 else 0)
        return targets[kind].at[pl.ds(pl.multiple_of(first, 64), rows), :]

    def source(kind, p):
        w = widths[kind]
        return sources[kind].at[:, pl.ds(pl.multiple_of(head_of(p) * w, w), w)]

    def in_copy(kind, p):
        return pltpu.make_async_remote_copy(
            src_ref=source(kind, p), dst_ref=target(kind, me),
            send_sem=in_send.at[kind, p], recv_sem=in_recv.at[kind, me],
            device_id=(seq, p), device_id_type=MESH,
        )

    def arrived(kind, j):
        pltpu.make_async_copy(target(kind, j), target(kind, j), in_recv.at[kind, j]).wait()

    for kind in range(4):
        pltpu.make_async_copy(source(kind, me), target(kind, me), in_recv.at[kind, me]).start()

    def clear(i, c):
        r = pl.multiple_of(i * BK, BK)
        dk[pl.ds(r, BK), :] = jnp.zeros((BK, HD), f32)
        dv[pl.ds(r, BK), :] = jnp.zeros((BK, HD), f32)
        return c

    lax.fori_loop(0, (WINDOW + group) // BK, clear, 0)

    pl.semaphore_wait(barrier, heads + 1)

    def send_all(first, lo, hi):
        def send(i, c):
            p = receiver(i)

            @pl.when(p != me)
            def _():
                in_copy(first, p).start()
                in_copy(first + 1, p).start()

            return c

        lax.fori_loop(lo, hi, send, 0)

    early = 10
    send_all(0, 0, heads)
    send_all(2, 0, early)

    def halo(i):
        ref = (kx, vx)[i]
        return pltpu.make_async_remote_copy(
            src_ref=ref.at[pl.ds(group, WINDOW), :], dst_ref=ref.at[pl.ds(0, WINDOW), :],
            send_sem=halo_send.at[i], recv_sem=halo_recv.at[i],
            device_id=next_id, device_id_type=MESH,
        )

    def kv_wait(j, c):
        arrived(0, j)
        arrived(1, j)
        return c

    late = (group - WINDOW) // rows
    lax.fori_loop(late, heads, kv_wait, 0)

    @pl.when(seq < groups - 1)
    def _():
        halo(0).start()
        halo(1).start()

    send_all(2, early, heads)
    lax.fori_loop(0, late, kv_wait, 0)

    def turn(i, c):
        r = pl.multiple_of(i * BK, BK)
        kt[:, pl.ds(r, BK)] = kx[pl.ds(r, BK), :].T
        return c

    lax.fori_loop(WINDOW // BK, (WINDOW + group) // BK, turn, 0)

    def halo_wait():
        @pl.when(seq == 0)
        def _():
            kx[pl.ds(0, WINDOW), :] = jnp.zeros((WINDOW, HD), bf16)
            vx[pl.ds(0, WINDOW), :] = jnp.zeros((WINDOW, HD), bf16)

        @pl.when(seq > 0)
        def _():
            for i, ref in enumerate((kx, vx)):
                own = ref.at[pl.ds(0, WINDOW), :]
                pltpu.make_async_copy(own, own, halo_recv.at[i]).wait()

        lax.fori_loop(0, WINDOW // BK, turn, 0)

    staged = (dqo, dko, dvo)
    results = (dq_hbm, dk_hbm, dv_hbm)

    def out_parts(kind, j):
        first = j * rows + (WINDOW if kind else 0)
        w = HD if kind else wide
        src = staged[kind].at[pl.ds(pl.multiple_of(first, 64), rows), :]
        return src, results[kind].at[:, pl.ds(pl.multiple_of(head_of(me) * w, w), w)]

    def out_copy(kind, j):
        src, dst = out_parts(kind, j)
        return pltpu.make_async_remote_copy(
            src_ref=src, dst_ref=dst,
            send_sem=out_send.at[kind, j], recv_sem=out_recv.at[kind, me],
            device_id=(seq, j), device_id_type=MESH,
        )

    def deliver(kinds, lo, count):
        def one(i, c):
            j = lo + lax.rem(i + place, count)
            for kind in kinds:
                @pl.when(j != me)
                def _():
                    out_copy(kind, j).start()

                @pl.when(j == me)
                def _():
                    src, dst = out_parts(kind, me)
                    pltpu.make_async_copy(src, dst, out_recv.at[kind, me]).start()

            return c

        lax.fori_loop(0, count, one, 0)

    def rim(i):
        return pltpu.make_async_remote_copy(
            src_ref=(dko, dvo)[i].at[pl.ds(0, WINDOW), :], dst_ref=(rk, rv)[i],
            send_sem=rim_send.at[i], recv_sem=rim_recv.at[i],
            device_id=prev_id, device_id_type=MESH,
        )

    def stage(lo, count):
        def one(i, c):
            r = pl.multiple_of(lo + i * 128, 128)
            dko[pl.ds(r, 128), :] = (dk[pl.ds(r, 128), :] * SCALE).astype(bf16)
            dvo[pl.ds(r, 128), :] = dv[pl.ds(r, 128), :].astype(bf16)
            return c

        lax.fori_loop(0, count // 128, one, 0)

    def at_stage(y, over):
        off = lax.rem(y - start + 2 * quads, quads)
        return jnp.where(off + over < quads, off + over, quads - 1)

    def step(n, c):
        quad = quad_at(n)

        def rows_wait(j, c):
            arrived(2, j)
            arrived(3, j)
            return c

        lax.fori_loop(quad * 4, quad * 4 + 4, rows_wait, 0)

        def tile(i, c):
            b = quad * per_quad + lax.rem(i + 1, per_quad)
            first_use = jnp.where(start == 1, per_quad, 1)

            @pl.when(b == first_use)
            def _():
                halo_wait()

            r = pl.multiple_of(b * BQ, BQ)
            qs = [qb[pl.ds(r, BQ), h * HD : (h + 1) * HD] for h in range(per)]
            dos = [dob[pl.ds(r, BQ), h * HD : (h + 1) * HD] for h in range(per)]
            grads = block(b, base, len_ref, qs, dos, kx, vx, kt, dk, dv, s_scr, p_scr)
            for h in range(per):
                dqo[pl.ds(r, BQ), h * HD : (h + 1) * HD] = grads[h].astype(bf16)
            return c

        lax.fori_loop(0, per_quad, tile, 0)
        @pl.when(n == at_stage(0, 1))
        def _():
            @pl.when(seq > 0)
            def _():
                stage(0, WINDOW)
                rim(0).start()
                rim(1).start()

        deliver((0,), quad * 4, 4)

        for y, count in ((0, 4), (1, 4), (2, late - 8)):
            @pl.when(n == at_stage(y, min(2, quads - 1 - y)))
            def _():
                stage(WINDOW + y * 4 * rows, count * rows)
                deliver((1, 2), y * 4, count)

        return c

    lax.fori_loop(0, quads, step, 0)

    @pl.when(seq < groups - 1)
    def _():
        for i, ref in enumerate((rk, rv)):
            pltpu.make_async_copy(ref, ref, rim_recv.at[i]).wait()

    def last(i, c):
        r = pl.multiple_of(group + i * 128, 128)
        o = pl.multiple_of(i * 128, 128)

        @pl.when(seq < groups - 1)
        def _():
            dk[pl.ds(r, 128), :] += rk[pl.ds(o, 128), :].astype(f32) * (1.0 / SCALE)
            dv[pl.ds(r, 128), :] += rv[pl.ds(o, 128), :].astype(f32)

        return c

    lax.fori_loop(0, WINDOW // 128, last, 0)
    stage(WINDOW + late * rows, (heads - late) * rows)
    deliver((1, 2), late, heads - late)

    def finish(t, c):
        p = peer(t)
        for kind in range(4):
            in_copy(kind, p).wait_send()
        for kind in range(3):
            out_copy(kind, p).wait_send()
        return c

    lax.fori_loop(1, heads, finish, 0)

    def landed(j, c):
        for kind in range(3):
            w = HD if kind else wide
            view = results[kind].at[:, pl.ds(pl.multiple_of(head_of(j) * w, w), w)]
            pltpu.make_async_copy(view, view, out_recv.at[kind, j]).wait()
        return c

    lax.fori_loop(0, heads, landed, 0)

    @pl.when(seq < groups - 1)
    def _():
        halo(0).wait_send()
        halo(1).wait_send()

    @pl.when(seq > 0)
    def _():
        rim(0).wait_send()
        rim(1).wait_send()


def local(queries, keys, values, grad_out, doc_lengths):
    heads, groups = lax.axis_size("head"), lax.axis_size("seq")
    rows = queries.shape[0]
    group = heads * rows
    ext = group + WINDOW
    per = queries.shape[1] // keys.shape[1]
    hbm = pl.BlockSpec(memory_space=pl.ANY)
    dma = pltpu.SemaphoreType.DMA
    return pl.pallas_call(
        functools.partial(exchange_kernel, heads, groups),
        out_shape=(
            jax.ShapeDtypeStruct(queries.shape, bf16),
            jax.ShapeDtypeStruct(keys.shape, bf16),
            jax.ShapeDtypeStruct(values.shape, bf16),
        ),
        in_specs=[pl.BlockSpec(memory_space=pltpu.SMEM), hbm, hbm, hbm, hbm],
        out_specs=(hbm, hbm, hbm),
        scratch_shapes=[
            pltpu.VMEM((group, per * HD), bf16),
            pltpu.VMEM((group, per * HD), bf16),
            pltpu.VMEM((ext, HD), bf16),
            pltpu.VMEM((ext, HD), bf16),
            pltpu.VMEM((HD, ext), bf16),
            pltpu.VMEM((ext, HD), f32),
            pltpu.VMEM((ext, HD), f32),
            pltpu.VMEM((group, per * HD), bf16),
            pltpu.VMEM((ext, HD), bf16),
            pltpu.VMEM((ext, HD), bf16),
            pltpu.VMEM((WINDOW, HD), bf16),
            pltpu.VMEM((WINDOW, HD), bf16),
            pltpu.VMEM((per, NT, BK, BQ), f32),
            pltpu.VMEM((per, NT, BK, BQ), f32),
            dma((4, heads)),
            dma((4, heads)),
            dma((3, heads)),
            dma((3, heads)),
            dma((2,)),
            dma((2,)),
            dma((2,)),
            dma((2,)),
        ],
        compiler_params=pltpu.CompilerParams(
            collective_id=0, has_side_effects=True, vmem_limit_bytes=60 << 20
        ),
    )(doc_lengths, queries, keys, values, grad_out)


def solution(mesh):
    rows = P(("seq", "head"), None)
    return jax.shard_map(
        local,
        mesh=mesh,
        in_specs=(rows, rows, rows, rows, P()),
        out_specs=(rows, rows, rows),
        check_vma=False,
    )
```

```python
import functools

import jax
import jax.numpy as jnp
from jax import lax
from jax.experimental import pallas as pl
from jax.experimental.pallas import tpu as pltpu
from jax.sharding import PartitionSpec as P

HD = 128
WINDOW = 1024
BQ = 256
BK = 256
NT=(WINDOW+BQ)//BK
SCALE=HD**-0.5
C2=SCALE*1.4426950408889634
NEG=-1e30
f32 = jnp.float32
bf16 = jnp.bfloat16
NTK=(((1,),(1,)),((),()))
NN=(((1,),(0,)),((),()))
def block(b, base, len_ref, qs, dos, k_ref, v_ref, kt_ref, dk_ref, dv_ref, s_scr, p_scr):
    per=len(qs)
    first = base + b*BQ - WINDOW
    qi = lax.broadcasted_iota(jnp.int32,(1,BQ),1)
    gpos = first + WINDOW + qi
    end = jnp.int32(0)
    start = jnp.zeros((1,BQ),jnp.int32)
    for d in range(16):
        end = end + len_ref[d]
        start = jnp.where(gpos >= end, end, start)
    lo = jnp.maximum(qi+1, start-first)
    ki = lax.broadcasted_iota(jnp.int32,(BK,BQ),0)
    rows=[pl.ds(pl.multiple_of(b*BQ + t*BK, BK),BK) for t in range(NT)]
    stats=[]
    for h in range(per):
        q,do=qs[h],dos[h]
        m = None
        for t in range(NT):
            s = lax.dot_general(k_ref[rows[t],:], q, NTK, preferred_element_type=f32)
            ok = ki >= lo - t*BK
            if t==NT-1:
                ok = ok & (ki <= lax.broadcasted_iota(jnp.int32,(BK,BQ),1))
            s = jnp.where(ok, s, NEG)
            s_scr[h,t] = s
            mt = jnp.max(s.reshape(BK//8,8,BQ),axis=0)
            m = mt if m is None else jnp.maximum(m,mt)
        m = jnp.max(m,axis=0,keepdims=True)
        l = jnp.zeros((8,BQ),f32); dd = jnp.zeros((8,BQ),f32)
        for t in range(NT):
            p = jnp.exp2((s_scr[h,t]-m)*C2)
            s_scr[h,t] = p
            dp = lax.dot_general(v_ref[rows[t],:], do, NTK, preferred_element_type=f32)
            p_scr[h,t] = dp
            l = l + jnp.sum(p.reshape(BK//8,8,BQ),axis=0)
            dd = dd + jnp.sum((p*dp).reshape(BK//8,8,BQ),axis=0)
        l = jnp.sum(l,axis=0,keepdims=True); dd = jnp.sum(dd,axis=0,keepdims=True)
        inv = 1.0/l
        stats.append((inv,dd*inv))
    dqt = [None]*per
    q_all=jnp.concatenate(qs,axis=0); do_all=jnp.concatenate(dos,axis=0)
    for t in range(NT):
        ws=[];dss=[]
        for h in range(per):
            inv,dd=stats[h]
            w = s_scr[h,t]*inv
            ds = (w*(p_scr[h,t]-dd)).astype(bf16)
            ws.append(w.astype(bf16)); dss.append(ds)
            x = lax.dot_general(kt_ref[:,rows[t]], ds, NN, preferred_element_type=f32)
            dqt[h] = x if dqt[h] is None else dqt[h] + x
        dv_ref[rows[t],:] += lax.dot_general(jnp.concatenate(ws,axis=1), do_all, NN, preferred_element_type=f32)
        dk_ref[rows[t],:] += lax.dot_general(jnp.concatenate(dss,axis=1), q_all, NN, preferred_element_type=f32)
    return [(x*SCALE).T for x in dqt]


def exchange_kernel(
    heads, groups,
    len_ref, q_hbm, k_hbm, v_hbm, do_hbm,
    dq_hbm, dk_hbm, dv_hbm,
    qb, dob, kx, vx, kt, dk, dv, dqo, dko, dvo, rk, rv, s_scr, p_scr,
    in_send, in_recv, out_send, out_recv, halo_send, halo_recv, rim_send, rim_recv,
):
    rows = q_hbm.shape[0]
    group = heads * rows
    tiles = group // BQ
    per = q_hbm.shape[1] // k_hbm.shape[1]
    wide = per * HD
    me = lax.axis_index("head")
    seq = lax.axis_index("seq")
    base = seq * group
    MESH = pl.DeviceIdType.MESH

    quads = heads // 4
    per_quad = tiles // quads
    mine, place = me // 4, lax.rem(me, 4)

    def turned(to):
        return to // 2 + 2 * lax.rem(to, 2)

    start = lax.rem(mine + 1 + turned(place), quads)

    def quad_at(n):
        return lax.rem(start + n, quads)

    def receiver(i):
        to = lax.rem(place + lax.rem(i, 4), 4)
        return lax.rem(mine + 3 * quads - 1 - turned(to) - i // 4, quads) * 4 + to

    def peer(t):
        return lax.rem(me + t, heads)

    half = groups // 2

    def traded(p, yes):
        return p + lax.rem(p, 2) * yes * (2 - 4 * lax.rem(p // 2, 2))

    def head_of(p):
        return traded(p, seq // half)

    after = lax.rem(seq + 1, groups)
    before = lax.rem(seq + groups - 1, groups)
    next_id = (after, traded(me, lax.rem(seq // half + after // half, 2)))
    prev_id = (before, traded(me, lax.rem(seq // half + before // half, 2)))

    barrier = pltpu.get_barrier_semaphore()

    def greet(t, c):
        pl.semaphore_signal(barrier, inc=1, device_id=(seq, peer(t)), device_id_type=MESH)
        return c

    lax.fori_loop(1, heads, greet, 0)
    for near in (next_id, prev_id):
        pl.semaphore_signal(barrier, inc=1, device_id=near, device_id_type=MESH)

    sources = (k_hbm, v_hbm, q_hbm, do_hbm)
    targets = (kx, vx, qb, dob)
    widths = (HD, HD, wide, wide)

    def target(kind, j):
        first = j * rows + (WINDOW if kind < 2 else 0)
        return targets[kind].at[pl.ds(pl.multiple_of(first, 64), rows), :]

    def source(kind, p):
        w = widths[kind]
        return sources[kind].at[:, pl.ds(pl.multiple_of(head_of(p) * w, w), w)]

    def in_copy(kind, p):
        return pltpu.make_async_remote_copy(
            src_ref=source(kind, p), dst_ref=target(kind, me),
            send_sem=in_send.at[kind, p], recv_sem=in_recv.at[kind, me],
            device_id=(seq, p), device_id_type=MESH,
        )

    def arrived(kind, j):
        pltpu.make_async_copy(target(kind, j), target(kind, j), in_recv.at[kind, j]).wait()

    for kind in range(4):
        pltpu.make_async_copy(source(kind, me), target(kind, me), in_recv.at[kind, me]).start()

    pl.semaphore_wait(barrier, heads + 1)

    def send_all(first, lo, hi):
        def send(i, c):
            p = receiver(i)

            @pl.when(p != me)
            def _():
                in_copy(first, p).start()
                in_copy(first + 1, p).start()

            return c

        lax.fori_loop(lo, hi, send, 0)

    early = 10
    send_all(0, 0, heads)
    send_all(2, 0, early)

    def clear(i, c):
        r = pl.multiple_of(i * BK, BK)
        dk[pl.ds(r, BK), :] = jnp.zeros((BK, HD), f32)
        dv[pl.ds(r, BK), :] = jnp.zeros((BK, HD), f32)
        return c

    lax.fori_loop(0, (WINDOW + group) // BK, clear, 0)

    def halo(i):
        ref = (kx, vx)[i]
        return pltpu.make_async_remote_copy(
            src_ref=ref.at[pl.ds(group, WINDOW), :], dst_ref=ref.at[pl.ds(0, WINDOW), :],
            send_sem=halo_send.at[i], recv_sem=halo_recv.at[i],
            device_id=next_id, device_id_type=MESH,
        )

    def kv_wait(j, c):
        arrived(0, j)
        arrived(1, j)
        return c

    late = (group - WINDOW) // rows
    lax.fori_loop(late, heads, kv_wait, 0)

    @pl.when(seq < groups - 1)
    def _():
        halo(0).start()
        halo(1).start()

    send_all(2, early, heads)
    lax.fori_loop(0, late, kv_wait, 0)

    def turn(i, c):
        r = pl.multiple_of(i * BK, BK)
        kt[:, pl.ds(r, BK)] = kx[pl.ds(r, BK), :].T
        return c

    lax.fori_loop(WINDOW // BK, (WINDOW + group) // BK, turn, 0)

    def halo_wait():
        @pl.when(seq == 0)
        def _():
            kx[pl.ds(0, WINDOW), :] = jnp.zeros((WINDOW, HD), bf16)
            vx[pl.ds(0, WINDOW), :] = jnp.zeros((WINDOW, HD), bf16)

        @pl.when(seq > 0)
        def _():
            for i, ref in enumerate((kx, vx)):
                own = ref.at[pl.ds(0, WINDOW), :]
                pltpu.make_async_copy(own, own, halo_recv.at[i]).wait()

        lax.fori_loop(0, WINDOW // BK, turn, 0)

    staged = (dqo, dko, dvo)
    results = (dq_hbm, dk_hbm, dv_hbm)

    def out_parts(kind, j):
        first = j * rows + (WINDOW if kind else 0)
        w = HD if kind else wide
        src = staged[kind].at[pl.ds(pl.multiple_of(first, 64), rows), :]
        return src, results[kind].at[:, pl.ds(pl.multiple_of(head_of(me) * w, w), w)]

    def out_copy(kind, j):
        src, dst = out_parts(kind, j)
        return pltpu.make_async_remote_copy(
            src_ref=src, dst_ref=dst,
            send_sem=out_send.at[kind, j], recv_sem=out_recv.at[kind, me],
            device_id=(seq, j), device_id_type=MESH,
        )

    def deliver_to(kinds, j):
        for kind in kinds:
            @pl.when(j != me)
            def _():
                out_copy(kind, j).start()

            @pl.when(j == me)
            def _():
                src, dst = out_parts(kind, me)
                pltpu.make_async_copy(src, dst, out_recv.at[kind, me]).start()

    def deliver(kinds, lo, count):
        def one(i, c):
            deliver_to(kinds, lo + lax.rem(i + place, count))
            return c

        lax.fori_loop(0, count, one, 0)

    def rim(i):
        return pltpu.make_async_remote_copy(
            src_ref=(dko, dvo)[i].at[pl.ds(0, WINDOW), :], dst_ref=(rk, rv)[i],
            send_sem=rim_send.at[i], recv_sem=rim_recv.at[i],
            device_id=prev_id, device_id_type=MESH,
        )

    def stage(lo, count):
        def one(i, c):
            r = pl.multiple_of(lo + i * 128, 128)
            dko[pl.ds(r, 128), :] = (dk[pl.ds(r, 128), :] * SCALE).astype(bf16)
            dvo[pl.ds(r, 128), :] = dv[pl.ds(r, 128), :].astype(bf16)
            return c

        lax.fori_loop(0, count // 128, one, 0)

    def at_stage(y, over):
        off = lax.rem(y - start + 2 * quads, quads)
        return jnp.where(off + over < quads, off + over, quads - 1)

    def whole_at(y):
        return at_stage(y, jnp.minimum(2, quads - 1 - y))

    def in_turn(wanted):
        def one(i, c):
            j = quad_at(lax.rem(i, 4)) * 4 + lax.rem(place + i // 4 + lax.rem(i, 4), 4)

            @pl.when(wanted(j))
            def _():
                deliver_to((1, 2), j)

            return c

        lax.fori_loop(0, heads, one, 0)

    def step(n, c):
        quad = quad_at(n)

        def rows_wait(j, c):
            arrived(2, j)
            arrived(3, j)
            return c

        lax.fori_loop(quad * 4, quad * 4 + 4, rows_wait, 0)

        def tile(i, c):
            b = quad * per_quad + lax.rem(i + 1, per_quad)
            first_use = jnp.where(start == 1, per_quad, 1)

            @pl.when(b == first_use)
            def _():
                halo_wait()

            r = pl.multiple_of(b * BQ, BQ)
            qs = [qb[pl.ds(r, BQ), h * HD : (h + 1) * HD] for h in range(per)]
            dos = [dob[pl.ds(r, BQ), h * HD : (h + 1) * HD] for h in range(per)]
            grads = block(b, base, len_ref, qs, dos, kx, vx, kt, dk, dv, s_scr, p_scr)
            for h in range(per):
                dqo[pl.ds(r, BQ), h * HD : (h + 1) * HD] = grads[h].astype(bf16)
            return c

        lax.fori_loop(0, per_quad, tile, 0)
        @pl.when(n == at_stage(0, 1))
        def _():
            @pl.when(seq > 0)
            def _():
                stage(0, WINDOW)
                rim(0).start()
                rim(1).start()

        deliver((0,), quad * 4, 4)

        for y, count in ((0, 4), (1, 4), (2, late - 8)):
            @pl.when(n == whole_at(y))
            def _():
                stage(WINDOW + y * 4 * rows, count * rows)

                @pl.when(n < quads - 1)
                def _():
                    deliver((1, 2), y * 4, count)

        return c

    lax.fori_loop(0, quads, step, 0)

    in_turn(lambda j: (j < late) & (whole_at(j // 4) == quads - 1))

    @pl.when(seq < groups - 1)
    def _():
        for i, ref in enumerate((rk, rv)):
            pltpu.make_async_copy(ref, ref, rim_recv.at[i]).wait()

    def last(i, c):
        r = pl.multiple_of(group + i * 128, 128)
        o = pl.multiple_of(i * 128, 128)

        @pl.when(seq < groups - 1)
        def _():
            dk[pl.ds(r, 128), :] += rk[pl.ds(o, 128), :].astype(f32) * (1.0 / SCALE)
            dv[pl.ds(r, 128), :] += rv[pl.ds(o, 128), :].astype(f32)

        return c

    lax.fori_loop(0, WINDOW // 128, last, 0)
    stage(WINDOW + late * rows, (heads - late) * rows)
    in_turn(lambda j: j >= late)

    def finish(t, c):
        p = peer(t)
        for kind in range(4):
            in_copy(kind, p).wait_send()
        for kind in range(3):
            out_copy(kind, p).wait_send()
        return c

    lax.fori_loop(1, heads, finish, 0)

    def landed(j, c):
        for kind in range(3):
            w = HD if kind else wide
            view = results[kind].at[:, pl.ds(pl.multiple_of(head_of(j) * w, w), w)]
            pltpu.make_async_copy(view, view, out_recv.at[kind, j]).wait()
        return c

    lax.fori_loop(0, heads, landed, 0)

    @pl.when(seq < groups - 1)
    def _():
        halo(0).wait_send()
        halo(1).wait_send()

    @pl.when(seq > 0)
    def _():
        rim(0).wait_send()
        rim(1).wait_send()


def local(queries, keys, values, grad_out, doc_lengths):
    heads, groups = lax.axis_size("head"), lax.axis_size("seq")
    rows = queries.shape[0]
    group = heads * rows
    ext = group + WINDOW
    per = queries.shape[1] // keys.shape[1]
    hbm = pl.BlockSpec(memory_space=pl.ANY)
    dma = pltpu.SemaphoreType.DMA
    return pl.pallas_call(
        functools.partial(exchange_kernel, heads, groups),
        out_shape=(
            jax.ShapeDtypeStruct(queries.shape, bf16),
            jax.ShapeDtypeStruct(keys.shape, bf16),
            jax.ShapeDtypeStruct(values.shape, bf16),
        ),
        in_specs=[pl.BlockSpec(memory_space=pltpu.SMEM), hbm, hbm, hbm, hbm],
        out_specs=(hbm, hbm, hbm),
        scratch_shapes=[
            pltpu.VMEM((group, per * HD), bf16),
            pltpu.VMEM((group, per * HD), bf16),
            pltpu.VMEM((ext, HD), bf16),
            pltpu.VMEM((ext, HD), bf16),
            pltpu.VMEM((HD, ext), bf16),
            pltpu.VMEM((ext, HD), f32),
            pltpu.VMEM((ext, HD), f32),
            pltpu.VMEM((group, per * HD), bf16),
            pltpu.VMEM((ext, HD), bf16),
            pltpu.VMEM((ext, HD), bf16),
            pltpu.VMEM((WINDOW, HD), bf16),
            pltpu.VMEM((WINDOW, HD), bf16),
            pltpu.VMEM((per, NT, BK, BQ), f32),
            pltpu.VMEM((per, NT, BK, BQ), f32),
            dma((4, heads)),
            dma((4, heads)),
            dma((3, heads)),
            dma((3, heads)),
            dma((2,)),
            dma((2,)),
            dma((2,)),
            dma((2,)),
        ],
        compiler_params=pltpu.CompilerParams(
            collective_id=0, has_side_effects=True, vmem_limit_bytes=60 << 20
        ),
    )(doc_lengths, queries, keys, values, grad_out)


def solution(mesh):
    rows = P(("seq", "head"), None)
    return jax.shard_map(
        local,
        mesh=mesh,
        in_specs=(rows, rows, rows, rows, P()),
        out_specs=(rows, rows, rows),
        check_vma=False,
    )
```

```python
import functools

import jax
import jax.numpy as jnp
from jax import lax
from jax.experimental import pallas as pl
from jax.experimental.pallas import tpu as pltpu
from jax.sharding import PartitionSpec as P

HD = 128
WINDOW = 1024
BQ = 256
BK = 256
NT=(WINDOW+BQ)//BK
SCALE=HD**-0.5
C2=SCALE*1.4426950408889634
NEG=-1e30
f32 = jnp.float32
bf16 = jnp.bfloat16
NTK=(((1,),(1,)),((),()))
NN=(((1,),(0,)),((),()))
def block(b, base, len_ref, qs, dos, k_ref, v_ref, kt_ref, dk_ref, dv_ref, s_scr, p_scr):
    per=len(qs)
    first = base + b*BQ - WINDOW
    qi = lax.broadcasted_iota(jnp.int32,(1,BQ),1)
    gpos = first + WINDOW + qi
    end = jnp.int32(0)
    start = jnp.zeros((1,BQ),jnp.int32)
    for d in range(16):
        end = end + len_ref[d]
        start = jnp.where(gpos >= end, end, start)
    lo = jnp.maximum(qi+1, start-first)
    ki = lax.broadcasted_iota(jnp.int32,(BK,BQ),0)
    rows=[pl.ds(pl.multiple_of(b*BQ + t*BK, BK),BK) for t in range(NT)]
    stats=[]
    ms=[]
    for h in range(per):
        q,do=qs[h],dos[h]
        m = None
        for t in range(NT):
            s = lax.dot_general(k_ref[rows[t],:], q, NTK, preferred_element_type=f32)
            ok = ki >= lo - t*BK
            if t==NT-1:
                ok = ok & (ki <= lax.broadcasted_iota(jnp.int32,(BK,BQ),1))
            s = jnp.where(ok, s, NEG)
            s_scr[h,t] = s
            mt = jnp.max(s.reshape(BK//8,8,BQ),axis=0)
            m = mt if m is None else jnp.maximum(m,mt)
        ms.append(jnp.max(m,axis=0,keepdims=True))
    for h in range(per):
        do = dos[h]
        m = ms[h]
        l = jnp.zeros((8,BQ),f32); dd = jnp.zeros((8,BQ),f32)
        for t in range(NT):
            p = jnp.exp2((s_scr[h,t]-m)*C2)
            s_scr[h,t] = p
            dp = lax.dot_general(v_ref[rows[t],:], do, NTK, preferred_element_type=f32)
            p_scr[h,t] = dp
            l = l + jnp.sum(p.reshape(BK//8,8,BQ),axis=0)
            dd = dd + jnp.sum((p*dp).reshape(BK//8,8,BQ),axis=0)
        l = jnp.sum(l,axis=0,keepdims=True); dd = jnp.sum(dd,axis=0,keepdims=True)
        inv = 1.0/l
        stats.append((inv,dd*inv))
    dqt = [None]*per
    q_all=jnp.concatenate(qs,axis=0); do_all=jnp.concatenate(dos,axis=0)
    for t in range(NT):
        ws=[];dss=[]
        for h in range(per):
            inv,dd=stats[h]
            w = s_scr[h,t]*inv
            ds = (w*(p_scr[h,t]-dd)).astype(bf16)
            ws.append(w.astype(bf16)); dss.append(ds)
            x = lax.dot_general(kt_ref[:,rows[t]], ds, NN, preferred_element_type=f32)
            dqt[h] = x if dqt[h] is None else dqt[h] + x
        dv_ref[rows[t],:] += lax.dot_general(jnp.concatenate(ws,axis=1), do_all, NN, preferred_element_type=f32)
        dk_ref[rows[t],:] += lax.dot_general(jnp.concatenate(dss,axis=1), q_all, NN, preferred_element_type=f32)
    return [(x*SCALE).T for x in dqt]


def exchange_kernel(
    heads, groups,
    len_ref, q_hbm, k_hbm, v_hbm, do_hbm,
    dq_hbm, dk_hbm, dv_hbm,
    qb, dob, kx, vx, kt, dk, dv, dqo, dko, dvo, rk, rv, s_scr, p_scr,
    in_send, in_recv, out_send, out_recv, halo_send, halo_recv, rim_send, rim_recv,
):
    rows = q_hbm.shape[0]
    group = heads * rows
    tiles = group // BQ
    per = q_hbm.shape[1] // k_hbm.shape[1]
    wide = per * HD
    me = lax.axis_index("head")
    seq = lax.axis_index("seq")
    base = seq * group
    MESH = pl.DeviceIdType.MESH

    quads = heads // 4
    per_quad = tiles // quads
    mine, place = me // 4, lax.rem(me, 4)

    def turned(to):
        return to // 2 + 2 * lax.rem(to, 2)

    start = lax.rem(mine + 1 + turned(place), quads)

    def quad_at(n):
        return lax.rem(start + n, quads)

    def receiver(i):
        to = lax.rem(place + lax.rem(i, 4), 4)
        return lax.rem(mine + 3 * quads - 1 - turned(to) - i // 4, quads) * 4 + to

    def peer(t):
        return lax.rem(me + t, heads)

    half = groups // 2

    def traded(p, yes):
        return p + lax.rem(p, 2) * yes * (2 - 4 * lax.rem(p // 2, 2))

    def head_of(p):
        return traded(p, seq // half)

    after = lax.rem(seq + 1, groups)
    before = lax.rem(seq + groups - 1, groups)
    next_id = (after, traded(me, lax.rem(seq // half + after // half, 2)))
    prev_id = (before, traded(me, lax.rem(seq // half + before // half, 2)))

    barrier = pltpu.get_barrier_semaphore()

    def greet(t, c):
        pl.semaphore_signal(barrier, inc=1, device_id=(seq, peer(t)), device_id_type=MESH)
        return c

    lax.fori_loop(1, heads, greet, 0)
    for near in (next_id, prev_id):
        pl.semaphore_signal(barrier, inc=1, device_id=near, device_id_type=MESH)

    sources = (k_hbm, v_hbm, q_hbm, do_hbm)
    targets = (kx, vx, qb, dob)
    widths = (HD, HD, wide, wide)

    def target(kind, j):
        first = j * rows + (WINDOW if kind < 2 else 0)
        return targets[kind].at[pl.ds(pl.multiple_of(first, 64), rows), :]

    def source(kind, p):
        w = widths[kind]
        return sources[kind].at[:, pl.ds(pl.multiple_of(head_of(p) * w, w), w)]

    def in_copy(kind, p):
        return pltpu.make_async_remote_copy(
            src_ref=source(kind, p), dst_ref=target(kind, me),
            send_sem=in_send.at[kind, p], recv_sem=in_recv.at[kind, me],
            device_id=(seq, p), device_id_type=MESH,
        )

    def arrived(kind, j):
        pltpu.make_async_copy(target(kind, j), target(kind, j), in_recv.at[kind, j]).wait()

    for kind in range(4):
        pltpu.make_async_copy(source(kind, me), target(kind, me), in_recv.at[kind, me]).start()

    pl.semaphore_wait(barrier, heads + 1)

    def send_all(first, lo, hi):
        def send(i, c):
            p = receiver(i)

            @pl.when(p != me)
            def _():
                in_copy(first, p).start()
                in_copy(first + 1, p).start()

            return c

        lax.fori_loop(lo, hi, send, 0)

    early = 10
    send_all(0, 0, heads)
    send_all(2, 0, early)

    def clear(i, c):
        r = pl.multiple_of(i * BK, BK)
        dk[pl.ds(r, BK), :] = jnp.zeros((BK, HD), f32)
        dv[pl.ds(r, BK), :] = jnp.zeros((BK, HD), f32)
        return c

    lax.fori_loop(0, (WINDOW + group) // BK, clear, 0)

    def halo(i):
        ref = (kx, vx)[i]
        return pltpu.make_async_remote_copy(
            src_ref=ref.at[pl.ds(group, WINDOW), :], dst_ref=ref.at[pl.ds(0, WINDOW), :],
            send_sem=halo_send.at[i], recv_sem=halo_recv.at[i],
            device_id=next_id, device_id_type=MESH,
        )

    def kv_wait(j, c):
        arrived(0, j)
        arrived(1, j)
        return c

    late = (group - WINDOW) // rows
    lax.fori_loop(late, heads, kv_wait, 0)

    @pl.when(seq < groups - 1)
    def _():
        halo(0).start()
        halo(1).start()

    send_all(2, early, heads)
    lax.fori_loop(0, late, kv_wait, 0)

    def turn(i, c):
        r = pl.multiple_of(i * BK, BK)
        kt[:, pl.ds(r, BK)] = kx[pl.ds(r, BK), :].T
        return c

    lax.fori_loop(WINDOW // BK, (WINDOW + group) // BK, turn, 0)

    def halo_wait():
        @pl.when(seq == 0)
        def _():
            kx[pl.ds(0, WINDOW), :] = jnp.zeros((WINDOW, HD), bf16)
            vx[pl.ds(0, WINDOW), :] = jnp.zeros((WINDOW, HD), bf16)

        @pl.when(seq > 0)
        def _():
            for i, ref in enumerate((kx, vx)):
                own = ref.at[pl.ds(0, WINDOW), :]
                pltpu.make_async_copy(own, own, halo_recv.at[i]).wait()

        lax.fori_loop(0, WINDOW // BK, turn, 0)

    staged = (dqo, dko, dvo)
    results = (dq_hbm, dk_hbm, dv_hbm)

    def out_parts(kind, j):
        first = j * rows + (WINDOW if kind else 0)
        w = HD if kind else wide
        src = staged[kind].at[pl.ds(pl.multiple_of(first, 64), rows), :]
        return src, results[kind].at[:, pl.ds(pl.multiple_of(head_of(me) * w, w), w)]

    def out_copy(kind, j):
        src, dst = out_parts(kind, j)
        return pltpu.make_async_remote_copy(
            src_ref=src, dst_ref=dst,
            send_sem=out_send.at[kind, j], recv_sem=out_recv.at[kind, me],
            device_id=(seq, j), device_id_type=MESH,
        )

    def deliver_to(kinds, j):
        for kind in kinds:
            @pl.when(j != me)
            def _():
                out_copy(kind, j).start()

            @pl.when(j == me)
            def _():
                src, dst = out_parts(kind, me)
                pltpu.make_async_copy(src, dst, out_recv.at[kind, me]).start()

    def deliver(kinds, lo, count):
        def one(i, c):
            deliver_to(kinds, lo + lax.rem(i + place, count))
            return c

        lax.fori_loop(0, count, one, 0)

    def rim(i):
        return pltpu.make_async_remote_copy(
            src_ref=(dko, dvo)[i].at[pl.ds(0, WINDOW), :], dst_ref=(rk, rv)[i],
            send_sem=rim_send.at[i], recv_sem=rim_recv.at[i],
            device_id=prev_id, device_id_type=MESH,
        )

    def stage(lo, count):
        def one(i, c):
            r = pl.multiple_of(lo + i * 128, 128)
            dko[pl.ds(r, 128), :] = (dk[pl.ds(r, 128), :] * SCALE).astype(bf16)
            dvo[pl.ds(r, 128), :] = dv[pl.ds(r, 128), :].astype(bf16)
            return c

        lax.fori_loop(0, count // 128, one, 0)

    def at_stage(y, over):
        off = lax.rem(y - start + 2 * quads, quads)
        return jnp.where(off + over < quads, off + over, quads - 1)

    def whole_at(y):
        return at_stage(y, jnp.minimum(2, quads - 1 - y))

    def in_turn(wanted):
        def one(i, c):
            j = quad_at(lax.rem(i, 4)) * 4 + lax.rem(place + i // 4 + lax.rem(i, 4), 4)

            @pl.when(wanted(j))
            def _():
                deliver_to((1, 2), j)

            return c

        lax.fori_loop(0, heads, one, 0)

    def step(n, c):
        quad = quad_at(n)

        def rows_wait(j, c):
            arrived(2, j)
            arrived(3, j)
            return c

        lax.fori_loop(quad * 4, quad * 4 + 4, rows_wait, 0)

        def tile(i, c):
            b = quad * per_quad + lax.rem(i + 1, per_quad)
            first_use = jnp.where(start == 1, per_quad, 1)

            @pl.when(b == first_use)
            def _():
                halo_wait()

            r = pl.multiple_of(b * BQ, BQ)
            qs = [qb[pl.ds(r, BQ), h * HD : (h + 1) * HD] for h in range(per)]
            dos = [dob[pl.ds(r, BQ), h * HD : (h + 1) * HD] for h in range(per)]
            grads = block(b, base, len_ref, qs, dos, kx, vx, kt, dk, dv, s_scr, p_scr)
            for h in range(per):
                dqo[pl.ds(r, BQ), h * HD : (h + 1) * HD] = grads[h].astype(bf16)
            return c

        lax.fori_loop(0, per_quad, tile, 0)
        @pl.when(n == at_stage(0, 1))
        def _():
            @pl.when(seq > 0)
            def _():
                stage(0, WINDOW)
                rim(0).start()
                rim(1).start()

        deliver((0,), quad * 4, 4)

        for y, count in ((0, 4), (1, 4), (2, late - 8)):
            @pl.when(n == whole_at(y))
            def _():
                stage(WINDOW + y * 4 * rows, count * rows)

                @pl.when(n < quads - 1)
                def _():
                    deliver((1, 2), y * 4, count)

        return c

    lax.fori_loop(0, quads, step, 0)

    in_turn(lambda j: (j < late) & (whole_at(j // 4) == quads - 1))

    @pl.when(seq < groups - 1)
    def _():
        for i, ref in enumerate((rk, rv)):
            pltpu.make_async_copy(ref, ref, rim_recv.at[i]).wait()

    def last(i, c):
        r = pl.multiple_of(group + i * 128, 128)
        o = pl.multiple_of(i * 128, 128)

        @pl.when(seq < groups - 1)
        def _():
            dk[pl.ds(r, 128), :] += rk[pl.ds(o, 128), :].astype(f32) * (1.0 / SCALE)
            dv[pl.ds(r, 128), :] += rv[pl.ds(o, 128), :].astype(f32)

        return c

    lax.fori_loop(0, WINDOW // 128, last, 0)
    stage(WINDOW + late * rows, (heads - late) * rows)
    in_turn(lambda j: j >= late)

    def finish(t, c):
        p = peer(t)
        for kind in range(4):
            in_copy(kind, p).wait_send()
        for kind in range(3):
            out_copy(kind, p).wait_send()
        return c

    lax.fori_loop(1, heads, finish, 0)

    def landed(j, c):
        for kind in range(3):
            w = HD if kind else wide
            view = results[kind].at[:, pl.ds(pl.multiple_of(head_of(j) * w, w), w)]
            pltpu.make_async_copy(view, view, out_recv.at[kind, j]).wait()
        return c

    lax.fori_loop(0, heads, landed, 0)

    @pl.when(seq < groups - 1)
    def _():
        halo(0).wait_send()
        halo(1).wait_send()

    @pl.when(seq > 0)
    def _():
        rim(0).wait_send()
        rim(1).wait_send()


def local(queries, keys, values, grad_out, doc_lengths):
    heads, groups = lax.axis_size("head"), lax.axis_size("seq")
    rows = queries.shape[0]
    group = heads * rows
    ext = group + WINDOW
    per = queries.shape[1] // keys.shape[1]
    hbm = pl.BlockSpec(memory_space=pl.ANY)
    dma = pltpu.SemaphoreType.DMA
    return pl.pallas_call(
        functools.partial(exchange_kernel, heads, groups),
        out_shape=(
            jax.ShapeDtypeStruct(queries.shape, bf16),
            jax.ShapeDtypeStruct(keys.shape, bf16),
            jax.ShapeDtypeStruct(values.shape, bf16),
        ),
        in_specs=[pl.BlockSpec(memory_space=pltpu.SMEM), hbm, hbm, hbm, hbm],
        out_specs=(hbm, hbm, hbm),
        scratch_shapes=[
            pltpu.VMEM((group, per * HD), bf16),
            pltpu.VMEM((group, per * HD), bf16),
            pltpu.VMEM((ext, HD), bf16),
            pltpu.VMEM((ext, HD), bf16),
            pltpu.VMEM((HD, ext), bf16),
            pltpu.VMEM((ext, HD), f32),
            pltpu.VMEM((ext, HD), f32),
            pltpu.VMEM((group, per * HD), bf16),
            pltpu.VMEM((ext, HD), bf16),
            pltpu.VMEM((ext, HD), bf16),
            pltpu.VMEM((WINDOW, HD), bf16),
            pltpu.VMEM((WINDOW, HD), bf16),
            pltpu.VMEM((per, NT, BK, BQ), f32),
            pltpu.VMEM((per, NT, BK, BQ), f32),
            dma((4, heads)),
            dma((4, heads)),
            dma((3, heads)),
            dma((3, heads)),
            dma((2,)),
            dma((2,)),
            dma((2,)),
            dma((2,)),
        ],
        compiler_params=pltpu.CompilerParams(
            collective_id=0, has_side_effects=True, vmem_limit_bytes=60 << 20
        ),
    )(doc_lengths, queries, keys, values, grad_out)


def solution(mesh):
    rows = P(("seq", "head"), None)
    return jax.shard_map(
        local,
        mesh=mesh,
        in_specs=(rows, rows, rows, rows, P()),
        out_specs=(rows, rows, rows),
        check_vma=False,
    )
```

```python
import functools

import jax
import jax.numpy as jnp
from jax import lax
from jax.experimental import pallas as pl
from jax.experimental.pallas import tpu as pltpu
from jax.sharding import PartitionSpec as P

HD = 128
WINDOW = 1024
BQ = 256
BK = 256
NT=(WINDOW+BQ)//BK
SCALE=HD**-0.5
C2=SCALE*1.4426950408889634
NEG=-1e30
f32 = jnp.float32
bf16 = jnp.bfloat16
NTK=(((1,),(1,)),((),()))
NN=(((1,),(0,)),((),()))
def block(b, base, len_ref, qs, dos, k_ref, v_ref, kt_ref, dk_ref, dv_ref, s_scr, p_scr):
    per=len(qs)
    first = base + b*BQ - WINDOW
    qi = lax.broadcasted_iota(jnp.int32,(1,BQ),1)
    gpos = first + WINDOW + qi
    end = jnp.int32(0)
    start = jnp.zeros((1,BQ),jnp.int32)
    for d in range(16):
        end = end + len_ref[d]
        start = jnp.where(gpos >= end, end, start)
    lo = jnp.maximum(qi+1, start-first)
    ki = lax.broadcasted_iota(jnp.int32,(BK,BQ),0)
    rows=[pl.ds(pl.multiple_of(b*BQ + t*BK, BK),BK) for t in range(NT)]
    stats=[]
    ms=[]
    for h in range(per):
        q,do=qs[h],dos[h]
        m = None
        for t in range(NT):
            s = lax.dot_general(k_ref[rows[t],:], q, NTK, preferred_element_type=f32)
            ok = ki >= lo - t*BK
            if t==NT-1:
                ok = ok & (ki <= lax.broadcasted_iota(jnp.int32,(BK,BQ),1))
            s = jnp.where(ok, s, NEG)
            s_scr[h,t] = s
            mt = jnp.max(s.reshape(BK//8,8,BQ),axis=0)
            m = mt if m is None else jnp.maximum(m,mt)
        ms.append(jnp.max(m,axis=0,keepdims=True))
    for h in range(per):
        do = dos[h]
        m = ms[h]
        l = jnp.zeros((8,BQ),f32); dd = jnp.zeros((8,BQ),f32)
        for t in range(NT):
            p = jnp.exp2((s_scr[h,t]-m)*C2)
            s_scr[h,t] = p
            dp = lax.dot_general(v_ref[rows[t],:], do, NTK, preferred_element_type=f32)
            p_scr[h,t] = dp
            l = l + jnp.sum(p.reshape(BK//8,8,BQ),axis=0)
            dd = dd + jnp.sum((p*dp).reshape(BK//8,8,BQ),axis=0)
        l = jnp.sum(l,axis=0,keepdims=True); dd = jnp.sum(dd,axis=0,keepdims=True)
        inv = 1.0/l
        stats.append((inv,dd*inv))
    dqt = [None]*per
    q_all=jnp.concatenate(qs,axis=0); do_all=jnp.concatenate(dos,axis=0)
    for t in range(NT):
        ws=[];dss=[]
        for h in range(per):
            inv,dd=stats[h]
            w = s_scr[h,t]*inv
            ds = (w*(p_scr[h,t]-dd)).astype(bf16)
            ws.append(w.astype(bf16)); dss.append(ds)
            x = lax.dot_general(kt_ref[:,rows[t]], ds, NN, preferred_element_type=f32)
            dqt[h] = x if dqt[h] is None else dqt[h] + x
        dv_ref[rows[t],:] += lax.dot_general(jnp.concatenate(ws,axis=1), do_all, NN, preferred_element_type=f32)
        dk_ref[rows[t],:] += lax.dot_general(jnp.concatenate(dss,axis=1), q_all, NN, preferred_element_type=f32)
    return [(x*SCALE).T for x in dqt]


def exchange_kernel(
    heads, groups,
    len_ref, q_hbm, k_hbm, v_hbm, do_hbm,
    dq_hbm, dk_hbm, dv_hbm,
    qb, dob, kx, vx, kt, dk, dv, dqo, dko, dvo, rk, rv, s_scr, p_scr,
    in_send, in_recv, out_send, out_recv, halo_send, halo_recv, rim_send, rim_recv,
):
    rows = q_hbm.shape[0]
    group = heads * rows
    tiles = group // BQ
    per = q_hbm.shape[1] // k_hbm.shape[1]
    wide = per * HD
    me = lax.axis_index("head")
    seq = lax.axis_index("seq")
    base = seq * group
    MESH = pl.DeviceIdType.MESH

    quads = heads // 4
    per_quad = tiles // quads
    mine, place = me // 4, lax.rem(me, 4)

    def turned(to):
        return to // 2 + 2 * lax.rem(to, 2)

    start = lax.rem(mine + 1 + turned(place), quads)

    def quad_at(n):
        return lax.rem(start + n, quads)

    def receiver(i):
        to = lax.rem(place + lax.rem(i, 4), 4)
        return lax.rem(mine + 3 * quads - 1 - turned(to) - i // 4, quads) * 4 + to

    def peer(t):
        return lax.rem(me + t, heads)

    half = groups // 2

    def traded(p, yes):
        return p + lax.rem(p, 2) * yes * (2 - 4 * lax.rem(p // 2, 2))

    def head_of(p):
        return traded(p, seq // half)

    after = lax.rem(seq + 1, groups)
    before = lax.rem(seq + groups - 1, groups)
    next_id = (after, traded(me, lax.rem(seq // half + after // half, 2)))
    prev_id = (before, traded(me, lax.rem(seq // half + before // half, 2)))

    barrier = pltpu.get_barrier_semaphore()

    def greet(t, c):
        pl.semaphore_signal(barrier, inc=1, device_id=(seq, peer(t)), device_id_type=MESH)
        return c

    lax.fori_loop(1, heads, greet, 0)
    for near in (next_id, prev_id):
        pl.semaphore_signal(barrier, inc=1, device_id=near, device_id_type=MESH)

    sources = (k_hbm, v_hbm, q_hbm, do_hbm)
    targets = (kx, vx, qb, dob)
    widths = (HD, HD, wide, wide)

    def target(kind, j):
        first = j * rows + (WINDOW if kind < 2 else 0)
        return targets[kind].at[pl.ds(pl.multiple_of(first, 64), rows), :]

    def source(kind, p):
        w = widths[kind]
        return sources[kind].at[:, pl.ds(pl.multiple_of(head_of(p) * w, w), w)]

    def in_copy(kind, p):
        return pltpu.make_async_remote_copy(
            src_ref=source(kind, p), dst_ref=target(kind, me),
            send_sem=in_send.at[kind, p], recv_sem=in_recv.at[kind, me],
            device_id=(seq, p), device_id_type=MESH,
        )

    def arrived(kind, j):
        pltpu.make_async_copy(target(kind, j), target(kind, j), in_recv.at[kind, j]).wait()

    for kind in range(4):
        pltpu.make_async_copy(source(kind, me), target(kind, me), in_recv.at[kind, me]).start()

    pl.semaphore_wait(barrier, heads + 1)

    def send_all(first, lo, hi):
        def send(i, c):
            p = receiver(i)

            @pl.when(p != me)
            def _():
                in_copy(first, p).start()
                in_copy(first + 1, p).start()

            return c

        lax.fori_loop(lo, hi, send, 0)

    early = 8
    late = (group - WINDOW) // rows

    @pl.when(me >= late)
    def _():
        send_all(0, 0, heads)
        send_all(2, 0, early)

    @pl.when(me < late)
    def _():
        send_all(2, 0, 4)
        send_all(0, 0, heads)
        send_all(2, 4, early)

    def clear(i, c):
        r = pl.multiple_of(i * BK, BK)
        dk[pl.ds(r, BK), :] = jnp.zeros((BK, HD), f32)
        dv[pl.ds(r, BK), :] = jnp.zeros((BK, HD), f32)
        return c

    lax.fori_loop(0, (WINDOW + group) // BK, clear, 0)

    def halo(i):
        ref = (kx, vx)[i]
        return pltpu.make_async_remote_copy(
            src_ref=ref.at[pl.ds(group, WINDOW), :], dst_ref=ref.at[pl.ds(0, WINDOW), :],
            send_sem=halo_send.at[i], recv_sem=halo_recv.at[i],
            device_id=next_id, device_id_type=MESH,
        )

    def kv_wait(j, c):
        arrived(0, j)
        arrived(1, j)
        return c

    lax.fori_loop(late, heads, kv_wait, 0)

    @pl.when(seq < groups - 1)
    def _():
        halo(0).start()
        halo(1).start()

    send_all(2, early, heads)
    lax.fori_loop(0, late, kv_wait, 0)

    def turn(i, c):
        r = pl.multiple_of(i * BK, BK)
        kt[:, pl.ds(r, BK)] = kx[pl.ds(r, BK), :].T
        return c

    lax.fori_loop(WINDOW // BK, (WINDOW + group) // BK, turn, 0)

    def halo_wait():
        @pl.when(seq == 0)
        def _():
            kx[pl.ds(0, WINDOW), :] = jnp.zeros((WINDOW, HD), bf16)
            vx[pl.ds(0, WINDOW), :] = jnp.zeros((WINDOW, HD), bf16)

        @pl.when(seq > 0)
        def _():
            for i, ref in enumerate((kx, vx)):
                own = ref.at[pl.ds(0, WINDOW), :]
                pltpu.make_async_copy(own, own, halo_recv.at[i]).wait()

        lax.fori_loop(0, WINDOW // BK, turn, 0)

    staged = (dqo, dko, dvo)
    results = (dq_hbm, dk_hbm, dv_hbm)

    def out_parts(kind, j):
        first = j * rows + (WINDOW if kind else 0)
        w = HD if kind else wide
        src = staged[kind].at[pl.ds(pl.multiple_of(first, 64), rows), :]
        return src, results[kind].at[:, pl.ds(pl.multiple_of(head_of(me) * w, w), w)]

    def out_copy(kind, j):
        src, dst = out_parts(kind, j)
        return pltpu.make_async_remote_copy(
            src_ref=src, dst_ref=dst,
            send_sem=out_send.at[kind, j], recv_sem=out_recv.at[kind, me],
            device_id=(seq, j), device_id_type=MESH,
        )

    def deliver_to(kinds, j):
        for kind in kinds:
            @pl.when(j != me)
            def _():
                out_copy(kind, j).start()

            @pl.when(j == me)
            def _():
                src, dst = out_parts(kind, me)
                pltpu.make_async_copy(src, dst, out_recv.at[kind, me]).start()

    def deliver(kinds, lo, count):
        def one(i, c):
            deliver_to(kinds, lo + lax.rem(i + place, count))
            return c

        lax.fori_loop(0, count, one, 0)

    def rim(i):
        return pltpu.make_async_remote_copy(
            src_ref=(dko, dvo)[i].at[pl.ds(0, WINDOW), :], dst_ref=(rk, rv)[i],
            send_sem=rim_send.at[i], recv_sem=rim_recv.at[i],
            device_id=prev_id, device_id_type=MESH,
        )

    def stage(lo, count):
        def one(i, c):
            r = pl.multiple_of(lo + i * 128, 128)
            dko[pl.ds(r, 128), :] = (dk[pl.ds(r, 128), :] * SCALE).astype(bf16)
            dvo[pl.ds(r, 128), :] = dv[pl.ds(r, 128), :].astype(bf16)
            return c

        lax.fori_loop(0, count // 128, one, 0)

    def at_stage(y, over):
        off = lax.rem(y - start + 2 * quads, quads)
        return jnp.where(off + over < quads, off + over, quads - 1)

    def whole_at(y):
        return at_stage(y, jnp.minimum(2, quads - 1 - y))

    def in_turn(wanted):
        def one(i, c):
            j = quad_at(lax.rem(i, 4)) * 4 + lax.rem(place + i // 4 + lax.rem(i, 4), 4)

            @pl.when(wanted(j))
            def _():
                deliver_to((1, 2), j)

            return c

        lax.fori_loop(0, heads, one, 0)

    def step(n, c):
        quad = quad_at(n)

        def rows_wait(j, c):
            arrived(2, j)
            arrived(3, j)
            return c

        lax.fori_loop(quad * 4, quad * 4 + 4, rows_wait, 0)

        def tile(i, c):
            b = quad * per_quad + lax.rem(i + 1, per_quad)
            first_use = jnp.where(start == 1, per_quad, 1)

            @pl.when(b == first_use)
            def _():
                halo_wait()

            r = pl.multiple_of(b * BQ, BQ)
            qs = [qb[pl.ds(r, BQ), h * HD : (h + 1) * HD] for h in range(per)]
            dos = [dob[pl.ds(r, BQ), h * HD : (h + 1) * HD] for h in range(per)]
            grads = block(b, base, len_ref, qs, dos, kx, vx, kt, dk, dv, s_scr, p_scr)
            for h in range(per):
                dqo[pl.ds(r, BQ), h * HD : (h + 1) * HD] = grads[h].astype(bf16)
            return c

        lax.fori_loop(0, per_quad, tile, 0)
        @pl.when(n == at_stage(0, 1))
        def _():
            @pl.when(seq > 0)
            def _():
                stage(0, WINDOW)
                rim(0).start()
                rim(1).start()

        deliver((0,), quad * 4, 4)

        for y, count in ((0, 4), (1, 4), (2, late - 8)):
            @pl.when(n == whole_at(y))
            def _():
                stage(WINDOW + y * 4 * rows, count * rows)

                @pl.when(n < quads - 1)
                def _():
                    deliver((1, 2), y * 4, count)

        return c

    lax.fori_loop(0, quads, step, 0)

    in_turn(lambda j: (j < late) & (whole_at(j // 4) == quads - 1))

    @pl.when(seq < groups - 1)
    def _():
        for i, ref in enumerate((rk, rv)):
            pltpu.make_async_copy(ref, ref, rim_recv.at[i]).wait()

    def last(i, c):
        r = pl.multiple_of(group + i * 128, 128)
        o = pl.multiple_of(i * 128, 128)

        @pl.when(seq < groups - 1)
        def _():
            dk[pl.ds(r, 128), :] += rk[pl.ds(o, 128), :].astype(f32) * (1.0 / SCALE)
            dv[pl.ds(r, 128), :] += rv[pl.ds(o, 128), :].astype(f32)

        return c

    lax.fori_loop(0, WINDOW // 128, last, 0)
    stage(WINDOW + late * rows, (heads - late) * rows)
    in_turn(lambda j: j >= late)

    def finish(t, c):
        p = peer(t)
        for kind in range(4):
            in_copy(kind, p).wait_send()
        for kind in range(3):
            out_copy(kind, p).wait_send()
        return c

    lax.fori_loop(1, heads, finish, 0)

    def landed(j, c):
        for kind in range(3):
            w = HD if kind else wide
            view = results[kind].at[:, pl.ds(pl.multiple_of(head_of(j) * w, w), w)]
            pltpu.make_async_copy(view, view, out_recv.at[kind, j]).wait()
        return c

    lax.fori_loop(0, heads, landed, 0)

    @pl.when(seq < groups - 1)
    def _():
        halo(0).wait_send()
        halo(1).wait_send()

    @pl.when(seq > 0)
    def _():
        rim(0).wait_send()
        rim(1).wait_send()


def local(queries, keys, values, grad_out, doc_lengths):
    heads, groups = lax.axis_size("head"), lax.axis_size("seq")
    rows = queries.shape[0]
    group = heads * rows
    ext = group + WINDOW
    per = queries.shape[1] // keys.shape[1]
    hbm = pl.BlockSpec(memory_space=pl.ANY)
    dma = pltpu.SemaphoreType.DMA
    return pl.pallas_call(
        functools.partial(exchange_kernel, heads, groups),
        out_shape=(
            jax.ShapeDtypeStruct(queries.shape, bf16),
            jax.ShapeDtypeStruct(keys.shape, bf16),
            jax.ShapeDtypeStruct(values.shape, bf16),
        ),
        in_specs=[pl.BlockSpec(memory_space=pltpu.SMEM), hbm, hbm, hbm, hbm],
        out_specs=(hbm, hbm, hbm),
        scratch_shapes=[
            pltpu.VMEM((group, per * HD), bf16),
            pltpu.VMEM((group, per * HD), bf16),
            pltpu.VMEM((ext, HD), bf16),
            pltpu.VMEM((ext, HD), bf16),
            pltpu.VMEM((HD, ext), bf16),
            pltpu.VMEM((ext, HD), f32),
            pltpu.VMEM((ext, HD), f32),
            pltpu.VMEM((group, per * HD), bf16),
            pltpu.VMEM((ext, HD), bf16),
            pltpu.VMEM((ext, HD), bf16),
            pltpu.VMEM((WINDOW, HD), bf16),
            pltpu.VMEM((WINDOW, HD), bf16),
            pltpu.VMEM((per, NT, BK, BQ), f32),
            pltpu.VMEM((per, NT, BK, BQ), f32),
            dma((4, heads)),
            dma((4, heads)),
            dma((3, heads)),
            dma((3, heads)),
            dma((2,)),
            dma((2,)),
            dma((2,)),
            dma((2,)),
        ],
        compiler_params=pltpu.CompilerParams(
            collective_id=0, has_side_effects=True, vmem_limit_bytes=60 << 20
        ),
    )(doc_lengths, queries, keys, values, grad_out)


def solution(mesh):
    rows = P(("seq", "head"), None)
    return jax.shard_map(
        local,
        mesh=mesh,
        in_specs=(rows, rows, rows, rows, P()),
        out_specs=(rows, rows, rows),
        check_vma=False,
    )
```
